32 devices in a mesh: parts: 2 (over y), row: 4 (over z), col: 4 (over x, core).
Axes of the slice: x: 2, y: 2, z: 4, core: 2. Of those that a mesh axis runs over, the one named last changes fastest.
Arguments:
- single: bfloat16 [8, 1024, 768], P(None, ('parts', 'row'), 'col'), parts along dimension 1, may hold values from -6 to 6
- pair_act: bfloat16 [1024, 512, 128], P(('parts', 'row'), 'col'), parts along dimension 0, may hold values from -6 to 6
- token_mask: int32 [1024], P(('parts', 'row')), parts along dimension 0, may hold values 0 or 1
- atom_feats: bfloat16 [8192, 128], P(('parts', 'row', 'col')), parts along dimension 0, may hold values from -6 to 6
- atom_token: int32 [8192], P(('parts', 'row', 'col')), parts along dimension 0, may hold values from 0 to 127, as said below
- atom_count: int32 [32], P(('parts', 'row', 'col')), parts along dimension 0, may hold values from 32 to 256, as said below
- atom_weight: bfloat16 [128, 768], P(None, 'col'), may hold values from -0.5 to 0.5
- bias_weight: bfloat16 [128, 2, 16], replicated, may hold values from -16 to 16
- qkvg_weight: bfloat16 [2, 4, 768, 768], P(None, None, 'col'), may hold values from -0.21875 to 0.21875
- out_weight: bfloat16 [2, 768, 768], P(None, 'col'), may hold values from -0.21875 to 0.21875
Outputs:
- updated: bfloat16 [8, 1024, 768], P(None, ('parts', 'row'), 'col'), parts along dimension 1
The draws below stay inside these ranges and needn't reach their ends.
There are 2 independent parts, one for each index of `parts`. The reference program is written for one: setup_inputs(seed, part) draws one part's arguments, and reference() takes and returns one part's arrays. A program takes and returns all parts, laid end to end along the dimension named above; an argument that names none is the same for every part. Nothing has to cross between parts.
Inputs may be any that keep to these rules, and one draw needn't show every extreme that they name: `atom_token`: slots of a device hold atoms of the 128 tokens of that device's row block, numbered within the block; every token owns at least one live slot. The first atom_count slots of a device are live, the others are padding; in every draw some device has all 256 slots live.
All inputs are finite; a program needn't handle non-finite values. No bound on the sum of `token_mask` on one device may be relied on, other than what follows from the above.
Results may differ from the reference program's by a relative error of at most 0.014.
The reference program's roundings to bfloat16 on the way count: a program that leaves them out, or rounds other values in their place, can miss the bound.
Values may be sent and summed in bfloat16 or wider, within the bound.
A program may use at most 64 MiB of HBM per device.

```python
import math
import jax
import jax.numpy as jnp
from jax import lax

D = 768
HEADS = 16
HEAD_DIM = 48
CZ = 128
CA = 128
LAYERS = 2
SAMPLES = 8
TOK_DEV = 128
ATOM_DEV = 256
TOKENS = 512
GRID = 16
COL_DEVS = 4
TOK_COL = 32
ATOMS = 4096
N_ROW = 4


def draw_pair_act(key, part):
    drawn = jax.random.normal(jax.random.fold_in(key, 1), (TOKENS, TOKENS, CZ), jnp.float32)
    return jnp.clip(drawn, -6.0, 6.0).astype(jnp.bfloat16)


def draw_bias_weight(key, part):
    drawn = jnp.clip(jax.random.normal(jax.random.fold_in(key, 6), (CZ, LAYERS, HEADS), jnp.float32), -6.0, 6.0)
    base = drawn / math.sqrt(CZ)
    return base.astype(jnp.bfloat16)


def draw_atom_count(key, part):
    halvings = jax.random.randint(jax.random.fold_in(key, 11), (GRID,), 0, 4)
    counts = ATOM_DEV // jnp.left_shift(jnp.ones((GRID,), jnp.int32), halvings)
    counts = counts - jax.random.randint(jax.random.fold_in(key, 12), (GRID,), 0, max(ATOM_DEV // 16, 1))
    counts = jnp.maximum(counts, TOK_COL)
    fullest = jax.random.randint(jax.random.fold_in(key, 13), (), 0, GRID)
    return jnp.where(jnp.arange(GRID) == fullest, ATOM_DEV, counts).astype(jnp.int32)


def draw_atom_token(key, part):
    slot_ids = jnp.arange(ATOM_DEV, dtype=jnp.int32)
    column = jnp.arange(GRID, dtype=jnp.int32) % COL_DEVS
    assigned = column[:, None] * TOK_COL + slot_ids[None, :]
    scattered = jax.random.randint(jax.random.fold_in(key, 14), (GRID, ATOM_DEV), 0, TOK_DEV)
    return jnp.where(slot_ids[None, :] < TOK_COL, assigned, scattered).reshape(ATOMS).astype(jnp.int32)


def set_ends(result, key, least, top_value):
    longest = result.shape.index(max(result.shape))
    spots = []
    for shift in (0, 1):
        where = [jax.random.randint(jax.random.fold_in(key, axis), (), 0, length) for axis, length in enumerate(result.shape)]
        where[longest] = (where[longest] + shift) % result.shape[longest]
        spots.append(tuple(where))
    return result.at[spots[0]].set(least).at[spots[1]].set(top_value)


def block_scale(key, shape, cuts, least, high):
    factor_of, own = 1.0, jax.random.fold_in(key, 6)
    for position, shards_of in cuts:
        draws = jnp.exp(jax.random.uniform(jax.random.fold_in(own, position), (shards_of,), jnp.float32, least / len(cuts), high / len(cuts)))
        factor_of = factor_of * jnp.repeat(draws, shape[position] // shards_of).reshape([-1 if axis == position else 1 for axis in range(len(shape))])
    return factor_of


def normal_values(rng, dims, spread, limit, pieces=(), held_as=jnp.bfloat16):
    entries = spread * jax.random.normal(rng, dims, jnp.float32)
    if pieces:
        entries = entries * block_scale(rng, dims, pieces, -0.22, 0.18)
    return jnp.clip(entries, -limit, limit).astype(held_as)


def setup_inputs(seed: int = 0, part: int = 0) -> dict:
    key_of = jax.random.split(jax.random.key(seed), 11)
    own_keys = jax.random.split(jax.random.fold_in(key_of[10], part), 11)
    return {
        "single": normal_values(own_keys[0], (SAMPLES, TOKENS, D), 1.0, 6.0, ((1, 4), (2, 4))),
        "pair_act": draw_pair_act(jax.random.fold_in(jax.random.fold_in(key_of[10], part), 71), part),
        "token_mask": set_ends((jax.random.randint(own_keys[2], (TOKENS,), 0, 16) < 15).astype(jnp.int32), jax.random.fold_in(own_keys[2], 1), 0, 1),
        "atom_feats": normal_values(own_keys[3], (ATOMS, CA), 1.0, 6.0, ((0, 16),)),
        "atom_token": draw_atom_token(jax.random.fold_in(jax.random.fold_in(key_of[10], part), 71), part),
        "atom_count": draw_atom_count(jax.random.fold_in(jax.random.fold_in(key_of[10], part), 71), part),
        "atom_weight": normal_values(key_of[6], (CA, D), CA ** -0.5, 0.5, ((1, 4),)),
        "bias_weight": draw_bias_weight(jax.random.fold_in(key_of[10], 71), part),
        "qkvg_weight": normal_values(key_of[8], (LAYERS, 4, D, D), D ** -0.5, 0.21875, ((2, 4),)),
        "out_weight": normal_values(key_of[9], (LAYERS, D, D), D ** -0.5, 0.21875, ((1, 4),)),
    }


EPS = 1e-05
MASKED = -1000000000.0

def layer_norm(values):
    average = lax.optimization_barrier(jnp.mean(values, axis=-1, keepdims=True))
    centered = values - average
    variance = lax.optimization_barrier(jnp.mean(centered * centered, axis=-1, keepdims=True))
    return centered * lax.rsqrt(variance + EPS)

def reference(single, pair_act, token_mask, atom_feats, atom_token, atom_count, atom_weight, bias_weight, qkvg_weight, out_weight):
    slot_ids = jnp.arange(ATOMS, dtype=jnp.int32)
    device = slot_ids // ATOM_DEV
    live_slots = slot_ids % ATOM_DEV < atom_count[device]
    owners = (device // COL_DEVS * TOK_DEV + atom_token).astype(jnp.int32)
    live_float = live_slots.astype(jnp.float32)
    atom_sums = jax.ops.segment_sum(atom_feats.astype(jnp.float32) * live_float[:, None], owners, num_segments=TOKENS)
    counts = jax.ops.segment_sum(live_float, owners, num_segments=TOKENS)
    pooled = jnp.dot(atom_sums, atom_weight.astype(jnp.float32), precision=lax.Precision.HIGHEST) / counts[:, None]
    stream = (single.astype(jnp.float32) + pooled[None]).astype(jnp.bfloat16)

    def bias_rows(pair_block):
        normed_block = layer_norm(pair_block.astype(jnp.float32)).astype(jnp.bfloat16)
        return jnp.einsum('ijc,clh->lhij', normed_block.astype(jnp.float32), bias_weight.astype(jnp.float32)).astype(jnp.bfloat16)
    blocks = pair_act.reshape(N_ROW, TOK_DEV, TOKENS, CZ)
    biases = lax.map(bias_rows, blocks)
    biases = jnp.moveaxis(biases, 0, 2).reshape(LAYERS, HEADS, TOKENS, TOKENS)
    key_live = token_mask > 0
    score_scale = 1.0 / math.sqrt(HEAD_DIM)

    def head_attention(inputs):
        head_query, head_keys, head_values, head_bias = inputs
        scores = jnp.einsum('sqd,skd->sqk', head_query.astype(jnp.float32), head_keys.astype(jnp.float32)) * score_scale
        scores = scores + head_bias.astype(jnp.float32)[None]
        scores = jnp.where(key_live[None, None, :], scores, MASKED)
        highest = lax.optimization_barrier(jnp.max(scores, axis=-1, keepdims=True))
        exponent = jnp.exp(scores - highest)
        summed = lax.optimization_barrier(jnp.sum(exponent, axis=-1, keepdims=True))
        weights = exponent.astype(jnp.bfloat16)
        return jnp.einsum('sqk,skd->sqd', weights.astype(jnp.float32), head_values.astype(jnp.float32)) / summed
    for layer_idx in range(LAYERS):
        normed = layer_norm(stream.astype(jnp.float32)).astype(jnp.bfloat16)
        projected = jnp.einsum('std,fed->fste', normed.astype(jnp.float32), qkvg_weight[layer_idx].astype(jnp.float32))
        queries = projected[0].astype(jnp.bfloat16).reshape(SAMPLES, TOKENS, HEADS, HEAD_DIM).transpose(2, 0, 1, 3)
        key_rows = projected[1].astype(jnp.bfloat16).reshape(SAMPLES, TOKENS, HEADS, HEAD_DIM).transpose(2, 0, 1, 3)
        value_rows = projected[2].astype(jnp.bfloat16).reshape(SAMPLES, TOKENS, HEADS, HEAD_DIM).transpose(2, 0, 1, 3)
        gating = jax.nn.sigmoid(projected[3])
        attended = lax.map(head_attention, (queries, key_rows, value_rows, biases[layer_idx]))
        attended = attended.transpose(1, 2, 0, 3).reshape(SAMPLES, TOKENS, D)
        gated = (gating * attended).astype(jnp.bfloat16)
        update = jnp.einsum('std,ed->ste', gated.astype(jnp.float32), out_weight[layer_idx].astype(jnp.float32))
        stream = (stream.astype(jnp.float32) + update).astype(jnp.bfloat16)
    return stream
```

```python
import math

import jax
import jax.numpy as jnp
from jax import lax
from jax.experimental import pallas as pl
from jax.experimental.pallas import tpu as pltpu
from jax.sharding import PartitionSpec as P

HEAD_DIM = 48
LAYERS = 2


EPS = 1e-05
MASKED = -1000000000.0
START_LOW = -1e30


def layer_norm(values):
    average = jnp.mean(values, axis=-1, keepdims=True)
    centered = values - average
    variance = jnp.mean(centered * centered, axis=-1, keepdims=True)
    return centered * lax.rsqrt(variance + EPS)


def per_device(
    single,
    pair_act,
    token_mask,
    atom_feats,
    atom_token,
    atom_count,
    atom_weight,
    bias_weight,
    qkvg_weight,
    out_weight,
):
    tok_rows = single.shape[1]
    sample_count = single.shape[0]
    slot_ids = jnp.arange(atom_feats.shape[0], dtype=jnp.int32)
    live_slots = slot_ids < atom_count[0]
    token_ids = jnp.arange(tok_rows, dtype=jnp.int32)
    owner_match = (token_ids[:, None] == atom_token[None, :]) & live_slots[None, :]
    owners = owner_match.astype(jnp.float32)
    counts = jnp.sum(owners, axis=1)
    atom_sums = jnp.dot(
        owner_match.astype(jnp.bfloat16), atom_feats, preferred_element_type=jnp.float32
    )
    sum_total, count_total = (
        lax.psum(atom_sums.astype(jnp.bfloat16), "col").astype(jnp.float32),
        lax.psum(counts[:, None].astype(jnp.bfloat16), "col").astype(jnp.float32),
    )
    pooled = (
        jnp.dot(sum_total, atom_weight.astype(jnp.float32), precision=lax.Precision.HIGHEST)
        / count_total
    )
    stream = (single.astype(jnp.float32) + pooled[None]).astype(jnp.bfloat16)
    pair_normed = layer_norm(pair_act.astype(jnp.float32)).astype(jnp.bfloat16)
    biases = jnp.einsum(
        "ijc,clh->lhij", pair_normed, bias_weight, preferred_element_type=jnp.float32
    ).astype(jnp.bfloat16)
    live_keys = (token_mask > 0).astype(jnp.bfloat16)[None, :]
    score_scale = 1.0 / math.sqrt(HEAD_DIM)
    for layer_idx in range(LAYERS):
        spread = lax.all_to_all(biases[layer_idx], "col", split_axis=0, concat_axis=2, tiled=True)
        gathered = lax.all_gather(stream, "col", axis=2, tiled=True)
        normed = layer_norm(gathered.astype(jnp.float32)).astype(jnp.bfloat16)
        projected = jnp.einsum(
            "std,fed->fste", normed, qkvg_weight[layer_idx], preferred_element_type=jnp.float32
        )
        head_width = projected.shape[3]
        heads_here = head_width // HEAD_DIM
        queries = (
            projected[0].astype(jnp.bfloat16).reshape(sample_count, tok_rows, heads_here, HEAD_DIM)
        )
        key_rows = projected[1].astype(jnp.bfloat16)
        value_rows = projected[2].astype(jnp.bfloat16)
        gating = jax.nn.sigmoid(projected[3])

        def attend(running, incoming, offset, queries=queries, spread=spread):
            top_old, summed_old, acc_old = running
            keys_in, values_in, live_in = incoming
            key_count = keys_in.shape[1]
            keys_heads = keys_in.reshape(sample_count, key_count, heads_here, HEAD_DIM)
            values_heads = values_in.reshape(sample_count, key_count, heads_here, HEAD_DIM)
            scores = (
                jnp.einsum(
                    "sqhd,skhd->shqk", queries, keys_heads, preferred_element_type=jnp.float32
                )
                * score_scale
            )
            scores = scores + spread.astype(jnp.float32)[None]
            scores = jnp.where(live_in[0][None, None, None, :] > 0, scores, MASKED)
            top_new = jnp.maximum(top_old, jnp.max(scores, axis=-1))
            exponent = jnp.exp(scores - top_new[..., None])
            summed_new = jnp.sum(exponent, axis=-1)
            weights = exponent.astype(jnp.bfloat16)
            acc_new = jnp.einsum(
                "shqk,skhd->shqd", weights, values_heads, preferred_element_type=jnp.float32
            )
            return (top_new, summed_new, acc_new)

        start_state = (
            jnp.full((sample_count, heads_here, tok_rows), START_LOW, jnp.float32),
            jnp.zeros((sample_count, heads_here, tok_rows), jnp.float32),
            jnp.zeros((sample_count, heads_here, tok_rows, HEAD_DIM), jnp.float32),
        )
        top_end, summed_end, acc_end = attend(
            start_state,
            (
                lax.all_gather(key_rows, "row", axis=1, tiled=True),
                lax.all_gather(value_rows, "row", axis=1, tiled=True),
                lax.all_gather(live_keys, "row", axis=1, tiled=True),
            ),
            jnp.int32(0),
        )
        attended = acc_end / summed_end[..., None]
        attended = attended.transpose(0, 2, 1, 3).reshape(sample_count, tok_rows, head_width)
        gated = (gating * attended).astype(jnp.bfloat16)
        out_rows = out_weight[layer_idx]

        def project(summed, incoming, offset, out_rows=out_rows):
            return jnp.einsum("std,ed->ste", incoming, out_rows, preferred_element_type=jnp.float32)

        zero_update = jnp.zeros((sample_count, tok_rows, out_rows.shape[0]), jnp.float32)
        update = project(
            zero_update, lax.all_gather(gated, "col", axis=2, tiled=True), jnp.int32(0)
        )
        stream = (stream.astype(jnp.float32) + update).astype(jnp.bfloat16)
    return stream


MESH = pl.DeviceIdType.MESH
NT = (((1,), (1,)), ((), ()))


def remote(src, dst, send_sem, recv_sem, row, col):
    return pltpu.make_async_remote_copy(
        src_ref=src,
        dst_ref=dst,
        send_sem=send_sem,
        recv_sem=recv_sem,
        device_id={"row": row, "col": col},
        device_id_type=MESH,
    )


def fused(
    rows,
    cols,
    bias,
    single,
    feats,
    slot_token,
    slot_count,
    atom_weight,
    mask,
    qkvg,
    out_w,
    out,
    spread,
    stream,
    first,
    parts_buf,
    mask_buf,
    queries,
    keys,
    values,
    gates,
    gated,
    final,
    part_sems,
    mask_sems,
    a2a_sems,
    pair_sems,
    in_sems,
    ag_sems,
    swap_sems,
    gated_sems,
    end_sems,
):
    r = lax.axis_index("row")
    c = lax.axis_index("col")
    samples, width, tokens = single.shape
    group = samples // 2
    tasks = LAYERS * group
    full = width * cols
    heads = width // HEAD_DIM
    sibling = c + 1 - 2 * lax.rem(c, 2)
    across = lax.rem(c + 2, cols)
    far = lax.rem(sibling + 2, cols)
    side = lax.rem(r, 2)
    mine = lax.div(r, 2)
    other = 1 - mine
    near = r + 1 - 2 * side
    peer_rows = {1: near, 2: lax.rem(r + 2, rows), 3: lax.rem(near + 2, rows)}

    barrier = pltpu.get_barrier_semaphore()
    for dc in range(1, cols):
        pl.semaphore_signal(
            barrier,
            inc=1,
            device_id={"row": r, "col": lax.rem(c + dc, cols)},
            device_id_type=MESH,
        )
    for d in range(1, rows):
        pl.semaphore_signal(
            barrier, inc=1, device_id={"row": peer_rows[d], "col": c}, device_id_type=MESH
        )
    pl.semaphore_wait(barrier, cols - 1 + rows - 1)

    sent = []

    def begin(desc):
        desc.start()
        sent.append(desc)

    def col_of(d):
        return lax.rem(c + d, cols)

    def a2a_desc(l, d):
        to = col_of(d)
        return remote(
            bias.at[l, to],
            spread.at[l, side, c],
            a2a_sems.at[0, l, d],
            a2a_sems.at[1, l, d],
            r,
            to,
        )

    def a2a_arrived(l, d):
        frm = col_of(cols - d)
        remote(
            bias.at[l, frm],
            spread.at[l, side, frm],
            a2a_sems.at[0, l, d],
            a2a_sems.at[1, l, d],
            r,
            frm,
        ).wait_recv()

    def pair_desc(l, d):
        block = col_of(cols - d) if d else c
        src = spread.at[l, side, block] if d else bias.at[l, c]
        return remote(
            src,
            spread.at[l, side, block],
            pair_sems.at[0, l, d],
            pair_sems.at[1, l, d],
            near,
            c,
        )

    def pair_arrived(l, d):
        block = col_of(cols - d) if d else c
        remote(
            spread.at[l, 1 - side, block],
            spread.at[l, 1 - side, block],
            pair_sems.at[0, l, d],
            pair_sems.at[1, l, d],
            near,
            c,
        ).wait_recv()

    def bias_exchange(l):
        for d in (2, 3, 1):
            a2a_desc(l, d).start()
        pair_desc(l, 0).start()
        spread[l, side, c] = bias[l, c]

    def bias_pass(l):
        for d in (1, 2, 3):
            a2a_arrived(l, d)
            pair_desc(l, d).start()

    def bias_arrived(l):
        for d in range(cols):
            pair_arrived(l, d)

    for d in range(1, rows):
        begin(remote(mask, mask_buf.at[r], mask_sems.at[0, d], mask_sems.at[1, d], peer_rows[d], c))
    mask_buf[r] = mask[...]

    slots = feats.shape[0]
    token_ids = lax.broadcasted_iota(jnp.int32, (tokens, slots), 0)
    slot_ids = lax.broadcasted_iota(jnp.int32, (tokens, slots), 1)
    match = (token_ids == slot_token[...]) & (slot_ids < slot_count[...])
    owners = jnp.where(match, 1.0, 0.0).astype(jnp.bfloat16)
    parts_buf[c, 0:tokens] = jnp.dot(
        owners, feats[...], preferred_element_type=jnp.float32
    ).astype(jnp.bfloat16)
    parts_buf[c, tokens : tokens + 16] = lax.dot_general(
        jnp.ones((16, slots), jnp.bfloat16), owners, NT, preferred_element_type=jnp.float32
    ).astype(jnp.bfloat16)
    for d in range(1, cols):
        begin(
            remote(
                parts_buf.at[c],
                parts_buf.at[c],
                part_sems.at[0, d],
                part_sems.at[1, d],
                r,
                col_of(d),
            )
        )
    bias_exchange(0)
    for d in range(1, cols):
        frm = col_of(cols - d)
        remote(
            parts_buf.at[frm], parts_buf.at[frm], part_sems.at[0, d], part_sems.at[1, d], r, frm
        ).wait_recv()
    total = jnp.zeros((width, tokens), jnp.float32)
    count_row = jnp.zeros((1, tokens), jnp.float32)
    for k in range(cols):
        total = total + lax.dot_general(
            atom_weight[...], parts_buf[k, 0:tokens], NT, preferred_element_type=jnp.float32
        )
        count_row = count_row + parts_buf[k, tokens : tokens + 16].astype(jnp.float32)[0:1]
    pooled = total / count_row

    def in_desc(d, s):
        at = s + group * (side if d == 2 else 1 - side)
        return remote(
            first.at[at],
            stream.at[0, s, mine, c, side],
            in_sems.at[0, d, s],
            in_sems.at[1, d, s],
            peer_rows[d],
            c,
        )

    def in_arrived(d, s):
        half = mine if d == 1 else other
        block = side if d == 2 else 1 - side
        remote(
            first.at[s],
            stream.at[0, s, half, c, block],
            in_sems.at[0, d, s],
            in_sems.at[1, d, s],
            peer_rows[d],
            c,
        ).wait_recv()

    def start_sample(s):
        for k in range(2):
            at = s + group * k
            first[at] = (single[at].astype(jnp.float32) + pooled).astype(jnp.bfloat16)
        stream[0, s, mine, c, side] = first[s + group * side]
        for d in (1, 2, 3):
            begin(in_desc(d, s))

    def ag_desc(t, half, kind):
        l, s = lax.div(t, group), lax.rem(t, group)
        block = across if kind == 2 else c
        return remote(
            stream.at[l, s, half, block],
            stream.at[l, s, half, block],
            ag_sems.at[0, kind, t, half],
            ag_sems.at[1, kind, t, half],
            r,
            across if kind == 1 else sibling,
        )

    def ag_arrived(t, half, kind):
        l, s = lax.div(t, group), lax.rem(t, group)
        block = (sibling, across, far)[kind]
        remote(
            stream.at[l, s, half, block],
            stream.at[l, s, half, block],
            ag_sems.at[0, kind, t, half],
            ag_sems.at[1, kind, t, half],
            r,
            across if kind == 1 else sibling,
        ).wait_recv()

    def ag_send(t, half):
        ag_desc(t, half, 1).start()
        ag_desc(t, half, 0).start()

    def swap_desc(s):
        return remote(
            stream.at[1, s, mine, c],
            stream.at[1, s, mine, c],
            swap_sems.at[0, s],
            swap_sems.at[1, s],
            peer_rows[2],
            c,
        )

    def swap_arrived(s):
        remote(
            stream.at[1, s, other, c],
            stream.at[1, s, other, c],
            swap_sems.at[0, s],
            swap_sems.at[1, s],
            peer_rows[2],
            c,
        ).wait_recv()

    def stage(t):
        s = lax.rem(t, group)

        @pl.when(t < group)
        def _():
            in_arrived(1, s)
            ag_send(t, mine)
            in_arrived(2, s)
            in_arrived(3, s)
            ag_send(t, other)

        @pl.when(t >= group)
        def _():
            swap_arrived(s)
            ag_send(t, other)

    def forward(t):
        for half in (mine, other):
            ag_arrived(t, half, 1)
            ag_desc(t, half, 2).start()

    score_scale = 1.0 / math.sqrt(HEAD_DIM)

    def normed_half(l, s, half):
        here = jnp.concatenate(
            [
                jnp.concatenate([stream[l, s, half, k, b] for k in range(cols)], axis=0)
                for b in range(2)
            ],
            axis=1,
        ).astype(jnp.float32)
        average = jnp.mean(here, axis=0, keepdims=True)
        centered = here - average
        variance = jnp.mean(centered * centered, axis=0, keepdims=True)
        return (centered * lax.rsqrt(variance + EPS)).astype(jnp.bfloat16)

    def project(t):
        l, s = lax.div(t, group), lax.rem(t, group)
        for half in (mine, other):
            ag_arrived(t, half, 0)
            ag_arrived(t, half, 2)
            here = normed_half(l, s, half)

            def rows_of(f, here=here):
                return jnp.dot(qkvg[l, f], here, preferred_element_type=jnp.float32)

            keys[half] = rows_of(1).astype(jnp.bfloat16)
            values[half] = rows_of(2).astype(jnp.bfloat16)
            if half is mine:
                queries[...] = rows_of(0).T.astype(jnp.bfloat16)
                gates[...] = jax.nn.sigmoid(rows_of(3))

    def attend(t):
        l, s = lax.div(t, group), lax.rem(t, group)
        live = jnp.concatenate([mask_buf[k][0:1] for k in range(rows)], axis=1) > 0
        square = lax.broadcasted_iota(jnp.int32, (tokens, tokens), 0) == lax.broadcasted_iota(
            jnp.int32, (tokens, tokens), 1
        )
        for h in range(heads):
            at = slice(h * HEAD_DIM, (h + 1) * HEAD_DIM)
            key_here = jnp.concatenate([keys[k, at] for k in range(2)], axis=1)
            value_here = jnp.concatenate([values[k, at] for k in range(2)], axis=1)
            for b in range(2):
                cut = slice(b * tokens, (b + 1) * tokens)
                scores = (
                    jnp.dot(queries[cut, at], key_here, preferred_element_type=jnp.float32)
                    * score_scale
                )
                head_bias = jnp.concatenate([spread[l, b, k, h] for k in range(cols)], axis=1)
                scores = scores + head_bias.astype(jnp.float32)
                scores = jnp.where(live, scores, MASKED)
                highest = jnp.max(scores, axis=-1, keepdims=True)
                exponent = jnp.exp(scores - highest)
                summed = jnp.sum(exponent, axis=-1, keepdims=True)
                mixed = lax.dot_general(
                    value_here,
                    exponent.astype(jnp.bfloat16),
                    NT,
                    preferred_element_type=jnp.float32,
                )
                summed_row = jnp.sum(jnp.where(square, summed, 0.0), axis=0, keepdims=True)
                attended = mixed * (1.0 / summed_row)
                gated[l, s, c, at, cut] = (gates[at, cut] * attended).astype(jnp.bfloat16)

    def gated_desc(t, kind):
        l, s = lax.div(t, group), lax.rem(t, group)
        block = across if kind == 2 else c
        return remote(
            gated.at[l, s, block],
            gated.at[l, s, block],
            gated_sems.at[0, kind, t],
            gated_sems.at[1, kind, t],
            r,
            across if kind == 1 else sibling,
        )

    def gated_arrived(t, kind):
        l, s = lax.div(t, group), lax.rem(t, group)
        block = (sibling, across, far)[kind]
        remote(
            gated.at[l, s, block],
            gated.at[l, s, block],
            gated_sems.at[0, kind, t],
            gated_sems.at[1, kind, t],
            r,
            across if kind == 1 else sibling,
        ).wait_recv()

    def end_desc(s):
        return remote(
            final.at[s, 1 - side],
            out.at[side * group + s],
            end_sems.at[0, s],
            end_sems.at[1, s],
            near,
            c,
        )

    def finish(t):
        l, s = lax.div(t, group), lax.rem(t, group)
        gated_arrived(t, 1)
        gated_desc(t, 2).start()
        gated_arrived(t, 0)
        gated_arrived(t, 2)
        joined = jnp.concatenate([gated[l, s, k] for k in range(cols)], axis=0)
        update = jnp.dot(out_w[l], joined, preferred_element_type=jnp.float32)
        for b in range(2):
            cut = slice(b * tokens, (b + 1) * tokens)
            before = stream[l, s, mine, c, b].astype(jnp.float32)
            final[s, b] = (before + update[:, cut]).astype(jnp.bfloat16)

        @pl.when(l + 1 < LAYERS)
        def _():
            stream[1, s, mine, c] = final[s]
            swap_desc(s).start()
            ag_send(t + group, mine)

        @pl.when(l + 1 == LAYERS)
        def _():
            end_desc(s).start()
            out[side * group + s] = final[s, side]

    start_sample(0)
    start_sample(1)
    bias_pass(0)
    for s in range(2, group):
        start_sample(s)
    for d in range(1, rows):
        frm = peer_rows[d]
        remote(
            mask, mask_buf.at[frm], mask_sems.at[0, d], mask_sems.at[1, d], frm, c
        ).wait_recv()
    stage(jnp.int32(0))

    def step(t, carry):
        @pl.when(t + 1 < tasks)
        def _():
            stage(t + 1)

        @pl.when(t == 0)
        def _():
            bias_exchange(1)

        @pl.when(t < tasks)
        def _():
            forward(t)
            project(t)

        @pl.when(t == 0)
        def _():
            bias_arrived(0)

        @pl.when(t == group)
        def _():
            bias_arrived(1)

        @pl.when(t < tasks)
        def _():
            attend(t)
            gated_desc(t, 1).start()
            gated_desc(t, 0).start()

        @pl.when(t == 0)
        def _():
            bias_pass(1)

        @pl.when(t >= 1)
        def _():
            finish(t - 1)

        return carry

    lax.fori_loop(0, tasks + 1, step, 0)

    for s in range(group):
        place = (1 - side) * group + s
        remote(
            final.at[s, side], out.at[place], end_sems.at[0, s], end_sems.at[1, s], near, c
        ).wait_recv()

    for desc in sent:
        desc.wait_send()
    for l in range(LAYERS):
        for d in range(1, cols):
            a2a_desc(l, d).wait_send()
        for d in range(cols):
            pair_desc(l, d).wait_send()
    for s in range(group):
        swap_desc(s).wait_send()
        end_desc(s).wait_send()

    def drain(t, carry):
        for kind in range(3):
            for half in (mine, other):
                ag_desc(t, half, kind).wait_send()
            gated_desc(t, kind).wait_send()
        return carry

    lax.fori_loop(0, tasks, drain, 0)


def pair_bias(x_ref, w_ref, o_ref):
    lines, across, chans = x_ref.shape
    here = x_ref[...].reshape(lines * across, chans).astype(jnp.float32)
    rounded = layer_norm(here).astype(jnp.bfloat16)
    biases = lax.dot_general(w_ref[...], rounded, NT, preferred_element_type=jnp.float32)
    o_ref[...] = biases.reshape(w_ref.shape[0], lines, across).astype(jnp.bfloat16)


def per_device_fused(
    rows,
    cols,
    single,
    pair_act,
    token_mask,
    atom_feats,
    atom_token,
    atom_count,
    atom_weight,
    bias_weight,
    qkvg_weight,
    out_weight,
):
    samples, tokens, width = single.shape
    single = single.transpose(0, 2, 1)
    group = samples // 2
    heads = width // HEAD_DIM
    chans = atom_feats.shape[1]
    slots = atom_feats.shape[0]
    lines, pairs = 16, pair_act.shape[2]
    all_heads = bias_weight.shape[1] * bias_weight.shape[2]
    biases = pl.pallas_call(
        pair_bias,
        grid=(tokens // lines,),
        in_specs=[
            pl.BlockSpec((lines, tokens, pairs), lambda i: (i, 0, 0)),
            pl.BlockSpec((all_heads, pairs), lambda i: (0, 0)),
        ],
        out_specs=pl.BlockSpec((all_heads, lines, tokens), lambda i: (0, i, 0)),
        out_shape=jax.ShapeDtypeStruct((all_heads, tokens, tokens), jnp.bfloat16),
        name="pair_bias",
    )(pair_act, bias_weight.reshape(pairs, all_heads).T)
    biases = biases.reshape(LAYERS, cols, heads, tokens, tokens)
    mask = jnp.broadcast_to((token_mask > 0).astype(jnp.float32)[None, :], (8, tokens))
    bf16, f32 = jnp.bfloat16, jnp.float32
    dma = pltpu.SemaphoreType.DMA
    updated = pl.pallas_call(
        lambda *refs: fused(rows, cols, *refs),
        out_shape=jax.ShapeDtypeStruct(single.shape, bf16),
        in_specs=[pl.BlockSpec(memory_space=pltpu.VMEM)] * 9,
        out_specs=pl.BlockSpec(memory_space=pltpu.VMEM),
        scratch_shapes=[
            pltpu.VMEM((LAYERS, 2, cols, heads, tokens, tokens), bf16),
            pltpu.VMEM((LAYERS, group, 2, cols, 2, width, tokens), bf16),
            pltpu.VMEM((samples, width, tokens), bf16),
            pltpu.VMEM((cols, tokens + 16, chans), bf16),
            pltpu.VMEM((rows, 8, tokens), f32),
            pltpu.VMEM((2 * tokens, width), bf16),
            pltpu.VMEM((2, width, 2 * tokens), bf16),
            pltpu.VMEM((2, width, 2 * tokens), bf16),
            pltpu.VMEM((width, 2 * tokens), f32),
            pltpu.VMEM((LAYERS, group, cols, width, 2 * tokens), bf16),
            pltpu.VMEM((group, 2, width, tokens), bf16),
            dma((2, cols)),
            dma((2, rows)),
            dma((2, LAYERS, cols)),
            dma((2, LAYERS, cols)),
            dma((2, rows, group)),
            dma((2, 3, LAYERS * group, 2)),
            dma((2, group)),
            dma((2, 3, LAYERS * group)),
            dma((2, group)),
        ],
        compiler_params=pltpu.CompilerParams(
            collective_id=0, has_side_effects=True, vmem_limit_bytes=56 * 1024 * 1024
        ),
        name="fused_blocks",
    )(
        biases,
        single,
        atom_feats,
        atom_token.reshape(1, slots),
        atom_count.reshape(1, 1),
        atom_weight.T,
        mask,
        qkvg_weight,
        out_weight,
    )
    return updated.transpose(0, 2, 1)


def solution(mesh):
    rows, cols = mesh.shape["row"], mesh.shape["col"]
    placed = (
        P(None, ("parts", "row"), "col"),
        P(("parts", "row"), "col", None),
        P(("parts", "row")),
        P(("parts", "row", "col"), None),
        P(("parts", "row", "col")),
        P(("parts", "row", "col")),
        P(None, "col"),
        P(),
        P(None, None, "col", None),
        P(None, "col", None),
    )

    def body(single, *rest):
        pairs = rest[0].shape
        square = rows == cols == 4 and single.shape[0] % 4 == 0 and pairs[0] == pairs[1]
        square = square and pairs[0] % 128 == 0
        if square and single.shape[2] % HEAD_DIM == 0:
            return per_device_fused(rows, cols, single, *rest)
        return per_device(single, *rest)

    return jax.shard_map(
        body,
        mesh=mesh,
        in_specs=placed,
        out_specs=P(None, ("parts", "row"), "col"),
        check_vma=False,
    )
```

```python
import math

import jax
import jax.numpy as jnp
from jax import lax
from jax.experimental import pallas as pl
from jax.experimental.pallas import tpu as pltpu
from jax.sharding import PartitionSpec as P

HEAD_DIM = 48
LAYERS = 2
CHUNKS = 4


EPS = 1e-05
MASKED = -1000000000.0
START_LOW = -1e30


def layer_norm(values):
    average = jnp.mean(values, axis=-1, keepdims=True)
    centered = values - average
    variance = jnp.mean(centered * centered, axis=-1, keepdims=True)
    return centered * lax.rsqrt(variance + EPS)


def per_device(
    single,
    pair_act,
    token_mask,
    atom_feats,
    atom_token,
    atom_count,
    atom_weight,
    bias_weight,
    qkvg_weight,
    out_weight,
):
    tok_rows = single.shape[1]
    sample_count = single.shape[0]
    slot_ids = jnp.arange(atom_feats.shape[0], dtype=jnp.int32)
    live_slots = slot_ids < atom_count[0]
    token_ids = jnp.arange(tok_rows, dtype=jnp.int32)
    owner_match = (token_ids[:, None] == atom_token[None, :]) & live_slots[None, :]
    owners = owner_match.astype(jnp.float32)
    counts = jnp.sum(owners, axis=1)
    atom_sums = jnp.dot(
        owner_match.astype(jnp.bfloat16), atom_feats, preferred_element_type=jnp.float32
    )
    sum_total, count_total = (
        lax.psum(atom_sums.astype(jnp.bfloat16), "col").astype(jnp.float32),
        lax.psum(counts[:, None].astype(jnp.bfloat16), "col").astype(jnp.float32),
    )
    pooled = (
        jnp.dot(sum_total, atom_weight.astype(jnp.float32), precision=lax.Precision.HIGHEST)
        / count_total
    )
    stream = (single.astype(jnp.float32) + pooled[None]).astype(jnp.bfloat16)
    pair_normed = layer_norm(pair_act.astype(jnp.float32)).astype(jnp.bfloat16)
    biases = jnp.einsum(
        "ijc,clh->lhij", pair_normed, bias_weight, preferred_element_type=jnp.float32
    ).astype(jnp.bfloat16)
    live_keys = (token_mask > 0).astype(jnp.bfloat16)[None, :]
    score_scale = 1.0 / math.sqrt(HEAD_DIM)
    for layer_idx in range(LAYERS):
        spread = lax.all_to_all(biases[layer_idx], "col", split_axis=0, concat_axis=2, tiled=True)
        gathered = lax.all_gather(stream, "col", axis=2, tiled=True)
        normed = layer_norm(gathered.astype(jnp.float32)).astype(jnp.bfloat16)
        projected = jnp.einsum(
            "std,fed->fste", normed, qkvg_weight[layer_idx], preferred_element_type=jnp.float32
        )
        head_width = projected.shape[3]
        heads_here = head_width // HEAD_DIM
        queries = (
            projected[0].astype(jnp.bfloat16).reshape(sample_count, tok_rows, heads_here, HEAD_DIM)
        )
        key_rows = projected[1].astype(jnp.bfloat16)
        value_rows = projected[2].astype(jnp.bfloat16)
        gating = jax.nn.sigmoid(projected[3])

        def attend(running, incoming, offset, queries=queries, spread=spread):
            top_old, summed_old, acc_old = running
            keys_in, values_in, live_in = incoming
            key_count = keys_in.shape[1]
            keys_heads = keys_in.reshape(sample_count, key_count, heads_here, HEAD_DIM)
            values_heads = values_in.reshape(sample_count, key_count, heads_here, HEAD_DIM)
            scores = (
                jnp.einsum(
                    "sqhd,skhd->shqk", queries, keys_heads, preferred_element_type=jnp.float32
                )
                * score_scale
            )
            scores = scores + spread.astype(jnp.float32)[None]
            scores = jnp.where(live_in[0][None, None, None, :] > 0, scores, MASKED)
            top_new = jnp.maximum(top_old, jnp.max(scores, axis=-1))
            exponent = jnp.exp(scores - top_new[..., None])
            summed_new = jnp.sum(exponent, axis=-1)
            weights = exponent.astype(jnp.bfloat16)
            acc_new = jnp.einsum(
                "shqk,skhd->shqd", weights, values_heads, preferred_element_type=jnp.float32
            )
            return (top_new, summed_new, acc_new)

        start_state = (
            jnp.full((sample_count, heads_here, tok_rows), START_LOW, jnp.float32),
            jnp.zeros((sample_count, heads_here, tok_rows), jnp.float32),
            jnp.zeros((sample_count, heads_here, tok_rows, HEAD_DIM), jnp.float32),
        )
        top_end, summed_end, acc_end = attend(
            start_state,
            (
                lax.all_gather(key_rows, "row", axis=1, tiled=True),
                lax.all_gather(value_rows, "row", axis=1, tiled=True),
                lax.all_gather(live_keys, "row", axis=1, tiled=True),
            ),
            jnp.int32(0),
        )
        attended = acc_end / summed_end[..., None]
        attended = attended.transpose(0, 2, 1, 3).reshape(sample_count, tok_rows, head_width)
        gated = (gating * attended).astype(jnp.bfloat16)
        out_rows = out_weight[layer_idx]

        def project(summed, incoming, offset, out_rows=out_rows):
            return jnp.einsum("std,ed->ste", incoming, out_rows, preferred_element_type=jnp.float32)

        zero_update = jnp.zeros((sample_count, tok_rows, out_rows.shape[0]), jnp.float32)
        update = project(
            zero_update, lax.all_gather(gated, "col", axis=2, tiled=True), jnp.int32(0)
        )
        stream = (stream.astype(jnp.float32) + update).astype(jnp.bfloat16)
    return stream


MESH = pl.DeviceIdType.MESH
NT = (((1,), (1,)), ((), ()))


def remote(src, dst, send_sem, recv_sem, row, col):
    return pltpu.make_async_remote_copy(
        src_ref=src,
        dst_ref=dst,
        send_sem=send_sem,
        recv_sem=recv_sem,
        device_id={"row": row, "col": col},
        device_id_type=MESH,
    )


def fused(
    rows,
    cols,
    pair_hbm,
    bias_w,
    single,
    feats,
    slot_token,
    slot_count,
    atom_weight,
    mask,
    qkvg_hbm,
    out_w_hbm,
    out,
    pair,
    bias,
    qkvg,
    out_w,
    spread,
    stream,
    first,
    parts_buf,
    mask_buf,
    queries,
    keys,
    values,
    gates,
    gated,
    final,
    part_sems,
    mask_sems,
    a2a_sems,
    pair_sems,
    in_sems,
    ag_sems,
    swap_sems,
    gated_sems,
    end_sems,
    load_sems,
):
    r = lax.axis_index("row")
    c = lax.axis_index("col")
    samples, width, tokens = single.shape
    group = samples // 2
    tasks = LAYERS * group
    full = width * cols
    heads = width // HEAD_DIM
    sibling = c + 1 - 2 * lax.rem(c, 2)
    across = lax.rem(c + 2, cols)
    far = lax.rem(sibling + 2, cols)
    side = lax.rem(r, 2)
    mine = lax.div(r, 2)
    other = 1 - mine
    near = r + 1 - 2 * side
    peer_rows = {1: near, 2: lax.rem(r + 2, rows), 3: lax.rem(near + 2, rows)}

    lines = tokens // CHUNKS

    def load(k):
        if k < CHUNKS:
            at = pl.ds(k * lines, lines)
            return pltpu.make_async_copy(pair_hbm.at[at], pair.at[at], load_sems.at[k])
        src, dst = ((qkvg_hbm, qkvg), (out_w_hbm, out_w))[k - CHUNKS]
        return pltpu.make_async_copy(src, dst, load_sems.at[k])

    for k in range(CHUNKS + 2):
        load(k).start()

    barrier = pltpu.get_barrier_semaphore()
    for dc in range(1, cols):
        pl.semaphore_signal(
            barrier,
            inc=1,
            device_id={"row": r, "col": lax.rem(c + dc, cols)},
            device_id_type=MESH,
        )
    for d in range(1, rows):
        pl.semaphore_signal(
            barrier, inc=1, device_id={"row": peer_rows[d], "col": c}, device_id_type=MESH
        )
    sent = []

    def begin(desc):
        desc.start()
        sent.append(desc)

    def col_of(d):
        return lax.rem(c + d, cols)

    def rows_at(k):
        return pl.ds(k * lines, lines)

    def bias_chunk(k):
        load(k).wait()
        here = pair_normed(pair[rows_at(k)].reshape(lines * tokens, pair.shape[2]))
        made = lax.dot_general(bias_w[...], here, NT, preferred_element_type=jnp.float32)
        made = made.astype(jnp.bfloat16).reshape(LAYERS, cols, heads, lines, tokens)
        bias[:, :, :, rows_at(k)] = made

    def a2a_desc(l, d, k):
        to = col_of(d)
        return remote(
            bias.at[l, to, :, rows_at(k)],
            spread.at[l, side, c, :, rows_at(k)],
            a2a_sems.at[0, l, d, k],
            a2a_sems.at[1, l, d, k],
            r,
            to,
        )

    def a2a_arrived(l, d, k):
        frm = col_of(cols - d)
        remote(
            bias.at[l, frm, :, rows_at(k)],
            spread.at[l, side, frm, :, rows_at(k)],
            a2a_sems.at[0, l, d, k],
            a2a_sems.at[1, l, d, k],
            r,
            frm,
        ).wait_recv()

    def pair_desc(l, d, k):
        block = col_of(cols - d) if d else c
        held = spread.at[l, side, block, :, rows_at(k)]
        return remote(
            held if d else bias.at[l, c, :, rows_at(k)],
            held,
            pair_sems.at[0, l, d, k],
            pair_sems.at[1, l, d, k],
            near,
            c,
        )

    def pair_arrived(l, d, k):
        block = col_of(cols - d) if d else c
        held = spread.at[l, 1 - side, block, :, rows_at(k)]
        remote(held, held, pair_sems.at[0, l, d, k], pair_sems.at[1, l, d, k], near, c).wait_recv()

    def bias_exchange(l, k):
        for d in (2, 3, 1):
            a2a_desc(l, d, k).start()
        pair_desc(l, 0, k).start()
        spread[l, side, c, :, rows_at(k)] = bias[l, c, :, rows_at(k)]

    def bias_pass(l, k):
        for d in (1, 2, 3):
            a2a_arrived(l, d, k)
            pair_desc(l, d, k).start()

    def bias_arrived(l):
        for k in range(CHUNKS):
            for d in range(cols):
                pair_arrived(l, d, k)

    slots = feats.shape[0]
    token_ids = lax.broadcasted_iota(jnp.int32, (tokens, slots), 0)
    slot_ids = lax.broadcasted_iota(jnp.int32, (tokens, slots), 1)
    match = (token_ids == slot_token[...]) & (slot_ids < slot_count[...])
    owners = jnp.where(match, 1.0, 0.0).astype(jnp.bfloat16)
    parts_buf[c, 0:tokens] = jnp.dot(
        owners, feats[...], preferred_element_type=jnp.float32
    ).astype(jnp.bfloat16)
    parts_buf[c, tokens : tokens + 16] = lax.dot_general(
        jnp.ones((16, slots), jnp.bfloat16), owners, NT, preferred_element_type=jnp.float32
    ).astype(jnp.bfloat16)
    bias_chunk(0)
    pl.semaphore_wait(barrier, cols - 1 + rows - 1)
    for d in range(1, cols):
        begin(
            remote(
                parts_buf.at[c],
                parts_buf.at[c],
                part_sems.at[0, d],
                part_sems.at[1, d],
                r,
                col_of(d),
            )
        )
    for d in range(1, rows):
        begin(remote(mask, mask_buf.at[r], mask_sems.at[0, d], mask_sems.at[1, d], peer_rows[d], c))
    mask_buf[r] = mask[...]

    bias_exchange(0, 0)
    bias_chunk(1)
    bias_exchange(0, 1)
    for d in range(1, cols):
        frm = col_of(cols - d)
        remote(
            parts_buf.at[frm], parts_buf.at[frm], part_sems.at[0, d], part_sems.at[1, d], r, frm
        ).wait_recv()
    total = jnp.zeros((width, tokens), jnp.float32)
    count_row = jnp.zeros((1, tokens), jnp.float32)
    for k in range(cols):
        total = total + lax.dot_general(
            atom_weight[...], parts_buf[k, 0:tokens], NT, preferred_element_type=jnp.float32
        )
        count_row = count_row + parts_buf[k, tokens : tokens + 16].astype(jnp.float32)[0:1]
    pooled = total / count_row

    def in_desc(d, s):
        at = s + group * (side if d == 2 else 1 - side)
        return remote(
            first.at[at],
            stream.at[0, s, mine, c, side],
            in_sems.at[0, d, s],
            in_sems.at[1, d, s],
            peer_rows[d],
            c,
        )

    def in_arrived(d, s):
        half = mine if d == 1 else other
        block = side if d == 2 else 1 - side
        remote(
            first.at[s],
            stream.at[0, s, half, c, block],
            in_sems.at[0, d, s],
            in_sems.at[1, d, s],
            peer_rows[d],
            c,
        ).wait_recv()

    def start_sample(s):
        for k in range(2):
            at = s + group * k
            first[at] = (single[at].astype(jnp.float32) + pooled).astype(jnp.bfloat16)
        stream[0, s, mine, c, side] = first[s + group * side]
        for d in (1, 2, 3):
            begin(in_desc(d, s))

    def ag_desc(t, half, kind):
        l, s = lax.div(t, group), lax.rem(t, group)
        block = across if kind == 2 else c
        return remote(
            stream.at[l, s, half, block],
            stream.at[l, s, half, block],
            ag_sems.at[0, kind, t, half],
            ag_sems.at[1, kind, t, half],
            r,
            across if kind == 1 else sibling,
        )

    def ag_arrived(t, half, kind):
        l, s = lax.div(t, group), lax.rem(t, group)
        block = (sibling, across, far)[kind]
        remote(
            stream.at[l, s, half, block],
            stream.at[l, s, half, block],
            ag_sems.at[0, kind, t, half],
            ag_sems.at[1, kind, t, half],
            r,
            across if kind == 1 else sibling,
        ).wait_recv()

    def ag_send(t, half):
        ag_desc(t, half, 1).start()
        ag_desc(t, half, 0).start()

    def swap_desc(s):
        return remote(
            stream.at[1, s, mine, c],
            stream.at[1, s, mine, c],
            swap_sems.at[0, s],
            swap_sems.at[1, s],
            peer_rows[2],
            c,
        )

    def swap_arrived(s):
        remote(
            stream.at[1, s, other, c],
            stream.at[1, s, other, c],
            swap_sems.at[0, s],
            swap_sems.at[1, s],
            peer_rows[2],
            c,
        ).wait_recv()

    def stage(t):
        s = lax.rem(t, group)

        @pl.when(t < group)
        def _():
            in_arrived(1, s)
            ag_send(t, mine)
            in_arrived(2, s)
            in_arrived(3, s)
            ag_send(t, other)

        @pl.when(t >= group)
        def _():
            swap_arrived(s)
            ag_send(t, other)

    def forward(t):
        for half in (mine, other):
            ag_arrived(t, half, 1)
            ag_desc(t, half, 2).start()

    score_scale = 1.0 / math.sqrt(HEAD_DIM)

    def normed_half(l, s, half):
        here = jnp.concatenate(
            [
                jnp.concatenate([stream[l, s, half, k, b] for k in range(cols)], axis=0)
                for b in range(2)
            ],
            axis=1,
        ).astype(jnp.float32)
        average = jnp.mean(here, axis=0, keepdims=True)
        centered = here - average
        variance = jnp.mean(centered * centered, axis=0, keepdims=True)
        return (centered * lax.rsqrt(variance + EPS)).astype(jnp.bfloat16)

    def project(t):
        l, s = lax.div(t, group), lax.rem(t, group)
        for half in (mine, other):
            ag_arrived(t, half, 0)
            ag_arrived(t, half, 2)
            here = normed_half(l, s, half)

            def rows_of(f, here=here):
                return jnp.dot(qkvg[l, f], here, preferred_element_type=jnp.float32)

            keys[half] = rows_of(1).astype(jnp.bfloat16)
            values[half] = rows_of(2).astype(jnp.bfloat16)
            if half is mine:
                queries[...] = rows_of(0).T.astype(jnp.bfloat16)
                gates[...] = jax.nn.sigmoid(rows_of(3))

    def attend(t):
        l, s = lax.div(t, group), lax.rem(t, group)
        live = jnp.concatenate([mask_buf[k] for k in range(rows)], axis=1) > 0
        square = lax.broadcasted_iota(jnp.int32, (tokens, tokens), 0) == lax.broadcasted_iota(
            jnp.int32, (tokens, tokens), 1
        )
        for h in range(heads):
            at = slice(h * HEAD_DIM, (h + 1) * HEAD_DIM)
            key_here = jnp.concatenate([keys[k, at] for k in range(2)], axis=1)
            value_here = jnp.concatenate([values[k, at] for k in range(2)], axis=1)
            for b in range(2):
                cut = slice(b * tokens, (b + 1) * tokens)
                scores = (
                    jnp.dot(queries[cut, at], key_here, preferred_element_type=jnp.float32)
                    * score_scale
                )
                head_bias = jnp.concatenate([spread[l, b, k, h] for k in range(cols)], axis=1)
                scores = scores + head_bias.astype(jnp.float32)
                scores = jnp.where(live, scores, MASKED)
                highest = jnp.max(scores, axis=-1, keepdims=True)
                exponent = jnp.exp(scores - highest)
                summed = jnp.sum(exponent, axis=-1, keepdims=True)
                mixed = lax.dot_general(
                    value_here,
                    exponent.astype(jnp.bfloat16),
                    NT,
                    preferred_element_type=jnp.float32,
                )
                summed_row = jnp.sum(jnp.where(square, summed, 0.0), axis=0, keepdims=True)
                attended = mixed * (1.0 / summed_row)
                gated[l, s, c, at, cut] = (gates[at, cut] * attended).astype(jnp.bfloat16)

    def gated_desc(t, kind):
        l, s = lax.div(t, group), lax.rem(t, group)
        block = across if kind == 2 else c
        return remote(
            gated.at[l, s, block],
            gated.at[l, s, block],
            gated_sems.at[0, kind, t],
            gated_sems.at[1, kind, t],
            r,
            across if kind == 1 else sibling,
        )

    def gated_arrived(t, kind):
        l, s = lax.div(t, group), lax.rem(t, group)
        block = (sibling, across, far)[kind]
        remote(
            gated.at[l, s, block],
            gated.at[l, s, block],
            gated_sems.at[0, kind, t],
            gated_sems.at[1, kind, t],
            r,
            across if kind == 1 else sibling,
        ).wait_recv()

    def end_desc(s):
        return remote(
            final.at[s, 1 - side],
            out.at[side * group + s],
            end_sems.at[0, s],
            end_sems.at[1, s],
            near,
            c,
        )

    def finish(t):
        l, s = lax.div(t, group), lax.rem(t, group)
        gated_arrived(t, 1)
        gated_desc(t, 2).start()
        gated_arrived(t, 0)
        gated_arrived(t, 2)
        joined = jnp.concatenate([gated[l, s, k] for k in range(cols)], axis=0)
        update = jnp.dot(out_w[l], joined, preferred_element_type=jnp.float32)
        for b in range(2):
            cut = slice(b * tokens, (b + 1) * tokens)
            before = stream[l, s, mine, c, b].astype(jnp.float32)
            final[s, b] = (before + update[:, cut]).astype(jnp.bfloat16)

        @pl.when(l + 1 < LAYERS)
        def _():
            stream[1, s, mine, c] = final[s]
            swap_desc(s).start()
            ag_send(t + group, mine)

        @pl.when(l + 1 == LAYERS)
        def _():
            end_desc(s).start()
            out[side * group + s] = final[s, side]

    start_sample(0)
    for k in range(2, CHUNKS):
        bias_chunk(k)
        bias_exchange(0, k)
        bias_pass(0, k - 2)
    stage(jnp.int32(0))
    for k in range(CHUNKS - 2, CHUNKS):
        bias_pass(0, k)
    for s in range(1, group):
        start_sample(s)
    for k in range(CHUNKS):
        bias_exchange(1, k)
    for d in range(1, rows):
        frm = peer_rows[d]
        remote(
            mask, mask_buf.at[frm], mask_sems.at[0, d], mask_sems.at[1, d], frm, c
        ).wait_recv()
    load(CHUNKS).wait()
    load(CHUNKS + 1).wait()

    def step(t, carry):
        @pl.when(t + 1 < tasks)
        def _():
            stage(t + 1)

        @pl.when(t < tasks)
        def _():
            forward(t)
            project(t)

        @pl.when(t == 0)
        def _():
            bias_arrived(0)

        @pl.when(t == group)
        def _():
            bias_arrived(1)

        @pl.when(t < tasks)
        def _():
            attend(t)
            gated_desc(t, 1).start()
            gated_desc(t, 0).start()

        @pl.when(t == 0)
        def _():
            for k in range(CHUNKS):
                bias_pass(1, k)

        @pl.when(t >= 1)
        def _():
            finish(t - 1)

        return carry

    lax.fori_loop(0, tasks + 1, step, 0)

    for s in range(group):
        place = (1 - side) * group + s
        remote(
            final.at[s, side], out.at[place], end_sems.at[0, s], end_sems.at[1, s], near, c
        ).wait_recv()

    for desc in sent:
        desc.wait_send()
    for l in range(LAYERS):
        for k in range(CHUNKS):
            for d in range(1, cols):
                a2a_desc(l, d, k).wait_send()
            for d in range(cols):
                pair_desc(l, d, k).wait_send()
    for s in range(group):
        swap_desc(s).wait_send()
        end_desc(s).wait_send()

    def drain(t, carry):
        for kind in range(3):
            for half in (mine, other):
                ag_desc(t, half, kind).wait_send()
            gated_desc(t, kind).wait_send()
        return carry

    lax.fori_loop(0, tasks, drain, 0)


def pair_normed(rows_in):
    chans = rows_in.shape[1]
    if chans & (chans - 1):
        return layer_norm(rows_in.astype(jnp.float32)).astype(jnp.bfloat16)
    share = jnp.full((chans, chans), 1.0 / chans, jnp.bfloat16)
    average = jnp.dot(rows_in, share, preferred_element_type=jnp.float32)
    centered = rows_in.astype(jnp.float32) - average
    square = centered * centered
    high = square.astype(jnp.bfloat16)
    low = (square - high.astype(jnp.float32)).astype(jnp.bfloat16)
    variance = jnp.dot(
        jnp.concatenate([high, low], axis=1),
        jnp.concatenate([share, share], axis=0),
        preferred_element_type=jnp.float32,
    )
    return (centered * lax.rsqrt(variance + EPS)).astype(jnp.bfloat16)


def per_device_fused(
    rows,
    cols,
    single,
    pair_act,
    token_mask,
    atom_feats,
    atom_token,
    atom_count,
    atom_weight,
    bias_weight,
    qkvg_weight,
    out_weight,
):
    samples, tokens, width = single.shape
    single = single.transpose(0, 2, 1)
    group = samples // 2
    heads = width // HEAD_DIM
    chans = atom_feats.shape[1]
    slots = atom_feats.shape[0]
    pairs = pair_act.shape[2]
    all_heads = bias_weight.shape[1] * bias_weight.shape[2]
    bf16, f32 = jnp.bfloat16, jnp.float32
    dma = pltpu.SemaphoreType.DMA
    updated = pl.pallas_call(
        lambda *refs: fused(rows, cols, *refs),
        out_shape=jax.ShapeDtypeStruct(single.shape, bf16),
        in_specs=[pl.BlockSpec(memory_space=pl.ANY)]
        + [pl.BlockSpec(memory_space=pltpu.VMEM)] * 7
        + [pl.BlockSpec(memory_space=pl.ANY)] * 2,
        out_specs=pl.BlockSpec(memory_space=pltpu.VMEM),
        scratch_shapes=[
            pltpu.VMEM(pair_act.shape, bf16),
            pltpu.VMEM((LAYERS, cols, heads, tokens, tokens), bf16),
            pltpu.VMEM(qkvg_weight.shape, bf16),
            pltpu.VMEM(out_weight.shape, bf16),
            pltpu.VMEM((LAYERS, 2, cols, heads, tokens, tokens), bf16),
            pltpu.VMEM((LAYERS, group, 2, cols, 2, width, tokens), bf16),
            pltpu.VMEM((samples, width, tokens), bf16),
            pltpu.VMEM((cols, tokens + 16, chans), bf16),
            pltpu.VMEM((rows, 1, tokens), jnp.int32),
            pltpu.VMEM((2 * tokens, width), bf16),
            pltpu.VMEM((2, width, 2 * tokens), bf16),
            pltpu.VMEM((2, width, 2 * tokens), bf16),
            pltpu.VMEM((width, 2 * tokens), f32),
            pltpu.VMEM((LAYERS, group, cols, width, 2 * tokens), bf16),
            pltpu.VMEM((group, 2, width, tokens), bf16),
            dma((2, cols)),
            dma((2, rows)),
            dma((2, LAYERS, cols, CHUNKS)),
            dma((2, LAYERS, cols, CHUNKS)),
            dma((2, rows, group)),
            dma((2, 3, LAYERS * group, 2)),
            dma((2, group)),
            dma((2, 3, LAYERS * group)),
            dma((2, group)),
            dma((CHUNKS + 2,)),
        ],
        compiler_params=pltpu.CompilerParams(
            collective_id=0, has_side_effects=True, vmem_limit_bytes=56 * 1024 * 1024
        ),
        name="fused_blocks",
    )(
        pair_act,
        bias_weight.reshape(pairs, all_heads).T,
        single,
        atom_feats,
        atom_token.reshape(1, slots),
        atom_count.reshape(1, 1),
        atom_weight.T,
        token_mask.reshape(1, tokens),
        qkvg_weight,
        out_weight,
    )
    return updated.transpose(0, 2, 1)


def solution(mesh):
    rows, cols = mesh.shape["row"], mesh.shape["col"]
    placed = (
        P(None, ("parts", "row"), "col"),
        P(("parts", "row"), "col", None),
        P(("parts", "row")),
        P(("parts", "row", "col"), None),
        P(("parts", "row", "col")),
        P(("parts", "row", "col")),
        P(None, "col"),
        P(),
        P(None, None, "col", None),
        P(None, "col", None),
    )

    def body(single, *rest):
        pairs = rest[0].shape
        square = rows == cols == 4 and single.shape[0] % 4 == 0 and pairs[0] == pairs[1]
        square = square and pairs[0] % 128 == 0
        if square and single.shape[2] % HEAD_DIM == 0:
            return per_device_fused(rows, cols, single, *rest)
        return per_device(single, *rest)

    return jax.shard_map(
        body,
        mesh=mesh,
        in_specs=placed,
        out_specs=P(None, ("parts", "row"), "col"),
        check_vma=False,
    )
```

```python
import math

import jax
import jax.numpy as jnp
from jax import lax
from jax.experimental import pallas as pl
from jax.experimental.pallas import tpu as pltpu
from jax.sharding import PartitionSpec as P

HEAD_DIM = 48
LAYERS = 2
CHUNKS = 4
RELAYED = 0


EPS = 1e-05
MASKED = -1000000000.0
START_LOW = -1e30


def layer_norm(values):
    average = jnp.mean(values, axis=-1, keepdims=True)
    centered = values - average
    variance = jnp.mean(centered * centered, axis=-1, keepdims=True)
    return centered * lax.rsqrt(variance + EPS)


def per_device(
    single,
    pair_act,
    token_mask,
    atom_feats,
    atom_token,
    atom_count,
    atom_weight,
    bias_weight,
    qkvg_weight,
    out_weight,
):
    tok_rows = single.shape[1]
    sample_count = single.shape[0]
    slot_ids = jnp.arange(atom_feats.shape[0], dtype=jnp.int32)
    live_slots = slot_ids < atom_count[0]
    token_ids = jnp.arange(tok_rows, dtype=jnp.int32)
    owner_match = (token_ids[:, None] == atom_token[None, :]) & live_slots[None, :]
    owners = owner_match.astype(jnp.float32)
    counts = jnp.sum(owners, axis=1)
    atom_sums = jnp.dot(
        owner_match.astype(jnp.bfloat16), atom_feats, preferred_element_type=jnp.float32
    )
    sum_total, count_total = (
        lax.psum(atom_sums.astype(jnp.bfloat16), "col").astype(jnp.float32),
        lax.psum(counts[:, None].astype(jnp.bfloat16), "col").astype(jnp.float32),
    )
    pooled = (
        jnp.dot(sum_total, atom_weight.astype(jnp.float32), precision=lax.Precision.HIGHEST)
        / count_total
    )
    stream = (single.astype(jnp.float32) + pooled[None]).astype(jnp.bfloat16)
    pair_normed = layer_norm(pair_act.astype(jnp.float32)).astype(jnp.bfloat16)
    biases = jnp.einsum(
        "ijc,clh->lhij", pair_normed, bias_weight, preferred_element_type=jnp.float32
    ).astype(jnp.bfloat16)
    live_keys = (token_mask > 0).astype(jnp.bfloat16)[None, :]
    score_scale = 1.0 / math.sqrt(HEAD_DIM)
    for layer_idx in range(LAYERS):
        spread = lax.all_to_all(biases[layer_idx], "col", split_axis=0, concat_axis=2, tiled=True)
        gathered = lax.all_gather(stream, "col", axis=2, tiled=True)
        normed = layer_norm(gathered.astype(jnp.float32)).astype(jnp.bfloat16)
        projected = jnp.einsum(
            "std,fed->fste", normed, qkvg_weight[layer_idx], preferred_element_type=jnp.float32
        )
        head_width = projected.shape[3]
        heads_here = head_width // HEAD_DIM
        queries = (
            projected[0].astype(jnp.bfloat16).reshape(sample_count, tok_rows, heads_here, HEAD_DIM)
        )
        key_rows = projected[1].astype(jnp.bfloat16)
        value_rows = projected[2].astype(jnp.bfloat16)
        gating = jax.nn.sigmoid(projected[3])

        def attend(running, incoming, offset, queries=queries, spread=spread):
            top_old, summed_old, acc_old = running
            keys_in, values_in, live_in = incoming
            key_count = keys_in.shape[1]
            keys_heads = keys_in.reshape(sample_count, key_count, heads_here, HEAD_DIM)
            values_heads = values_in.reshape(sample_count, key_count, heads_here, HEAD_DIM)
            scores = (
                jnp.einsum(
                    "sqhd,skhd->shqk", queries, keys_heads, preferred_element_type=jnp.float32
                )
                * score_scale
            )
            scores = scores + spread.astype(jnp.float32)[None]
            scores = jnp.where(live_in[0][None, None, None, :] > 0, scores, MASKED)
            top_new = jnp.maximum(top_old, jnp.max(scores, axis=-1))
            exponent = jnp.exp(scores - top_new[..., None])
            summed_new = jnp.sum(exponent, axis=-1)
            weights = exponent.astype(jnp.bfloat16)
            acc_new = jnp.einsum(
                "shqk,skhd->shqd", weights, values_heads, preferred_element_type=jnp.float32
            )
            return (top_new, summed_new, acc_new)

        start_state = (
            jnp.full((sample_count, heads_here, tok_rows), START_LOW, jnp.float32),
            jnp.zeros((sample_count, heads_here, tok_rows), jnp.float32),
            jnp.zeros((sample_count, heads_here, tok_rows, HEAD_DIM), jnp.float32),
        )
        top_end, summed_end, acc_end = attend(
            start_state,
            (
                lax.all_gather(key_rows, "row", axis=1, tiled=True),
                lax.all_gather(value_rows, "row", axis=1, tiled=True),
                lax.all_gather(live_keys, "row", axis=1, tiled=True),
            ),
            jnp.int32(0),
        )
        attended = acc_end / summed_end[..., None]
        attended = attended.transpose(0, 2, 1, 3).reshape(sample_count, tok_rows, head_width)
        gated = (gating * attended).astype(jnp.bfloat16)
        out_rows = out_weight[layer_idx]

        def project(summed, incoming, offset, out_rows=out_rows):
            return jnp.einsum("std,ed->ste", incoming, out_rows, preferred_element_type=jnp.float32)

        zero_update = jnp.zeros((sample_count, tok_rows, out_rows.shape[0]), jnp.float32)
        update = project(
            zero_update, lax.all_gather(gated, "col", axis=2, tiled=True), jnp.int32(0)
        )
        stream = (stream.astype(jnp.float32) + update).astype(jnp.bfloat16)
    return stream


MESH = pl.DeviceIdType.MESH
NT = (((1,), (1,)), ((), ()))


def remote(src, dst, send_sem, recv_sem, row, col):
    return pltpu.make_async_remote_copy(
        src_ref=src,
        dst_ref=dst,
        send_sem=send_sem,
        recv_sem=recv_sem,
        device_id={"row": row, "col": col},
        device_id_type=MESH,
    )


def fused(
    rows,
    cols,
    pair_hbm,
    bias_w,
    single,
    feats,
    slot_token,
    slot_count,
    atom_weight,
    mask,
    qkvg_hbm,
    out_w_hbm,
    out,
    pair,
    bias,
    qkvg,
    out_w,
    spread,
    stream,
    first,
    parts_buf,
    pooled,
    mask_buf,
    queries,
    keys,
    values,
    gates,
    gated,
    final,
    part_sems,
    mask_sems,
    a2a_sems,
    pair_sems,
    in_sems,
    ag_sems,
    swap_sems,
    gated_sems,
    end_sems,
    load_sems,
):
    r = lax.axis_index("row")
    c = lax.axis_index("col")
    samples, width, tokens = single.shape
    group = samples // 2
    tasks = LAYERS * group
    full = width * cols
    heads = width // HEAD_DIM
    sibling = c + 1 - 2 * lax.rem(c, 2)
    across = lax.rem(c + 2, cols)
    side = lax.rem(r, 2)
    mine = lax.div(r, 2)
    other = 1 - mine
    near = r + 1 - 2 * side
    peer_rows = {1: near, 2: lax.rem(r + 2, rows), 3: lax.rem(near + 2, rows)}

    lines = tokens // CHUNKS

    def load(k):
        if k < CHUNKS:
            at = pl.ds(k * lines, lines)
            return pltpu.make_async_copy(pair_hbm.at[at], pair.at[at], load_sems.at[k])
        src, dst = ((qkvg_hbm, qkvg), (out_w_hbm, out_w))[k - CHUNKS]
        return pltpu.make_async_copy(src, dst, load_sems.at[k])

    for k in range(CHUNKS + 2):
        load(k).start()

    barrier = pltpu.get_barrier_semaphore()
    for dc in range(1, cols):
        pl.semaphore_signal(
            barrier,
            inc=1,
            device_id={"row": r, "col": lax.rem(c + dc, cols)},
            device_id_type=MESH,
        )
    for d in range(1, rows):
        pl.semaphore_signal(
            barrier, inc=1, device_id={"row": peer_rows[d], "col": c}, device_id_type=MESH
        )
    def col_of(d):
        return lax.rem(c + d, cols)

    def rows_at(k):
        return pl.ds(k * lines, lines)

    def bias_chunk(k):
        load(k).wait()
        here = pair_normed(pair[rows_at(k)].reshape(lines * tokens, pair.shape[2]))
        made = lax.dot_general(bias_w[...], here, NT, preferred_element_type=jnp.float32)
        made = made.astype(jnp.bfloat16).reshape(LAYERS, cols, heads, lines, tokens)
        bias[:, :, :, rows_at(k)] = made

    def settle(ref, sem):
        pltpu.make_async_copy(ref, ref, sem).wait()

    def a2a_desc(l, d, k):
        to = col_of(d)
        return remote(
            bias.at[l, to, :, rows_at(k)],
            spread.at[l, side, c, :, rows_at(k)],
            a2a_sems.at[l, CHUNKS],
            a2a_sems.at[l, k],
            r,
            to,
        )

    def pair_desc(l, d, k):
        block = col_of(cols - d) if d else c
        held = spread.at[l, side, block, :, rows_at(k)]
        return remote(
            held if d else bias.at[l, c, :, rows_at(k)],
            held,
            pair_sems.at[0, l],
            pair_sems.at[1, l],
            near,
            c,
        )

    def bias_exchange(l, k):
        for d in (2, 3, 1):
            a2a_desc(l, d, k).start()
        if l == 0:
            pair_desc(l, 0, k).start()
        spread[l, side, c, :, rows_at(k)] = bias[l, c, :, rows_at(k)]

    def bias_pass(l, k):
        if l:
            pair_desc(l, 0, k).start()
        settle(spread.at[l, side, pl.ds(0, cols - 1), :, rows_at(k)], a2a_sems.at[l, k])
        for d in range(1, cols):
            pair_desc(l, d, k).start()

    def bias_arrived(l):
        settle(spread.at[l, 1 - side], pair_sems.at[1, l])

    slots = feats.shape[0]
    token_ids = lax.broadcasted_iota(jnp.int32, (tokens, slots), 0)
    slot_ids = lax.broadcasted_iota(jnp.int32, (tokens, slots), 1)
    match = (token_ids == slot_token[...]) & (slot_ids < slot_count[...])
    owners = jnp.where(match, 1.0, 0.0).astype(jnp.bfloat16)
    parts_buf[c, 0:tokens] = jnp.dot(
        owners, feats[...], preferred_element_type=jnp.float32
    ).astype(jnp.bfloat16)
    parts_buf[c, tokens : tokens + 16] = lax.dot_general(
        jnp.ones((16, slots), jnp.bfloat16), owners, NT, preferred_element_type=jnp.float32
    ).astype(jnp.bfloat16)
    bias_chunk(0)
    pl.semaphore_wait(barrier, cols - 1 + rows - 1)
    for d in range(1, cols):
        remote(
            parts_buf.at[c], parts_buf.at[c], part_sems.at[0], part_sems.at[1], r, col_of(d)
        ).start()
    for d in range(1, rows):
        remote(mask, mask_buf.at[r], mask_sems.at[0], mask_sems.at[1], peer_rows[d], c).start()
    mask_buf[r] = mask[...]

    bias_exchange(0, 0)
    bias_chunk(1)
    bias_exchange(0, 1)
    settle(parts_buf.at[pl.ds(0, cols - 1)], part_sems.at[1])
    total = jnp.zeros((width, tokens), jnp.float32)
    count_row = jnp.zeros((1, tokens), jnp.float32)
    for k in range(cols):
        total = total + lax.dot_general(
            atom_weight[...], parts_buf[k, 0:tokens], NT, preferred_element_type=jnp.float32
        )
        count_row = count_row + parts_buf[k, tokens : tokens + 16].astype(jnp.float32)[0:1]
    pooled[...] = total / count_row

    def in_desc(d, s):
        at = s + group * (side if d == 2 else 1 - side)
        return remote(
            first.at[at],
            stream.at[0, s, mine, c, side],
            in_sems.at[2, 0],
            in_sems.at[min(d, 2) - 1, s],
            peer_rows[d],
            c,
        )

    def start_sample(s):
        for k in range(2):
            at = s + group * k
            first[at] = (single[at].astype(jnp.float32) + pooled[...]).astype(jnp.bfloat16)
        stream[0, s, mine, c, side] = first[s + group * side]
        for d in (1, 2, 3):
            in_desc(d, s).start()

    def ag_desc(t, half, kind):
        l, s = lax.div(t, group), lax.rem(t, group)
        block = across if kind == 2 else c
        return remote(
            stream.at[l, s, half, block],
            stream.at[l, s, half, block],
            ag_sems.at[t, 4],
            ag_sems.at[t, 2 * half + kind % 2],
            r,
            across if kind == 1 else sibling,
        )

    def ag_arrived(t, half, kind):
        l, s = lax.div(t, group), lax.rem(t, group)
        held = stream.at[l, s, half, across] if kind else stream.at[l, s, half, pl.ds(0, 2)]
        settle(held, ag_sems.at[t, 2 * half + kind])

    def ag_send(t, half):
        ag_desc(t, half, 1).start()
        ag_desc(t, half, 0).start()

    def swap_desc(s):
        return remote(
            stream.at[1, s, mine, c],
            stream.at[1, s, mine, c],
            swap_sems.at[group],
            swap_sems.at[s],
            peer_rows[2],
            c,
        )

    def relay_desc(t):
        held = stream.at[1, lax.rem(t, group), mine, across]
        return remote(
            held, held, ag_sems.at[t, 4], ag_sems.at[t, 2 * mine + 1], peer_rows[2], c
        )

    def stage_first(t, half):
        if half is mine:
            settle(first.at[0], in_sems.at[0, t])
        else:
            settle(stream.at[0, t, other, c], in_sems.at[1, t])
        ag_send(t, half)

    def stage_next(t):
        s = lax.rem(t, group)
        settle(stream.at[1, s, other, c], swap_sems.at[s])

        @pl.when(t < tasks - RELAYED)
        def _():
            ag_desc(t, other, 1).start()

        ag_desc(t, other, 0).start()

    def forward(t, half):
        ag_arrived(t, half, 1)
        ag_desc(t, half, 2).start()

    score_scale = 1.0 / math.sqrt(HEAD_DIM)

    def normed_half(l, s, half):
        here = jnp.concatenate(
            [
                jnp.concatenate([stream[l, s, half, k, b] for k in range(cols)], axis=0)
                for b in range(2)
            ],
            axis=1,
        ).astype(jnp.float32)
        average = jnp.mean(here, axis=0, keepdims=True)
        centered = here - average
        variance = jnp.mean(centered * centered, axis=0, keepdims=True)
        return (centered * lax.rsqrt(variance + EPS)).astype(jnp.bfloat16)

    def project(t):
        l, s = lax.div(t, group), lax.rem(t, group)
        for half in (mine, other):
            ag_arrived(t, half, 0)
            here = normed_half(l, s, half)

            def rows_of(f, here=here):
                return jnp.dot(qkvg[l, f], here, preferred_element_type=jnp.float32)

            keys[half] = rows_of(1).astype(jnp.bfloat16)
            values[half] = rows_of(2).astype(jnp.bfloat16)
            if half is mine:
                queries[...] = rows_of(0).T.astype(jnp.bfloat16)
                gates[...] = jax.nn.sigmoid(rows_of(3))

    def attend(t):
        l, s = lax.div(t, group), lax.rem(t, group)
        live = jnp.concatenate([mask_buf[k] for k in range(rows)], axis=1) > 0
        square = lax.broadcasted_iota(jnp.int32, (tokens, tokens), 0) == lax.broadcasted_iota(
            jnp.int32, (tokens, tokens), 1
        )
        for h in range(heads):
            at = slice(h * HEAD_DIM, (h + 1) * HEAD_DIM)
            key_here = jnp.concatenate([keys[k, at] for k in range(2)], axis=1)
            value_here = jnp.concatenate([values[k, at] for k in range(2)], axis=1)
            for b in range(2):
                cut = slice(b * tokens, (b + 1) * tokens)
                scores = (
                    jnp.dot(queries[cut, at], key_here, preferred_element_type=jnp.float32)
                    * score_scale
                )
                head_bias = jnp.concatenate([spread[l, b, k, h] for k in range(cols)], axis=1)
                scores = scores + head_bias.astype(jnp.float32)
                scores = jnp.where(live, scores, MASKED)
                highest = jnp.max(scores, axis=-1, keepdims=True)
                exponent = jnp.exp(scores - highest)
                summed = jnp.sum(exponent, axis=-1, keepdims=True)
                mixed = lax.dot_general(
                    value_here,
                    exponent.astype(jnp.bfloat16),
                    NT,
                    preferred_element_type=jnp.float32,
                )
                summed_row = jnp.sum(jnp.where(square, summed, 0.0), axis=0, keepdims=True)
                attended = mixed * (1.0 / summed_row)
                gated[l, s, c, at, cut] = (gates[at, cut] * attended).astype(jnp.bfloat16)

    def gated_desc(t, kind):
        l, s = lax.div(t, group), lax.rem(t, group)
        block = across if kind == 2 else c
        return remote(
            gated.at[l, s, block],
            gated.at[l, s, block],
            gated_sems.at[2, 0],
            gated_sems.at[kind % 2, t],
            r,
            across if kind == 1 else sibling,
        )

    def end_desc(s):
        return remote(
            final.at[s, 1 - side],
            out.at[side * group + s],
            end_sems.at[0],
            end_sems.at[1],
            near,
            c,
        )

    def pass_gated(t):
        l, s = lax.div(t, group), lax.rem(t, group)
        settle(gated.at[l, s, across], gated_sems.at[1, t])
        gated_desc(t, 2).start()

    def finish(t):
        l, s = lax.div(t, group), lax.rem(t, group)
        settle(gated.at[l, s, pl.ds(0, 2)], gated_sems.at[0, t])
        joined = jnp.concatenate([gated[l, s, k] for k in range(cols)], axis=0)
        update = jnp.dot(out_w[l], joined, preferred_element_type=jnp.float32)
        for b in range(2):
            cut = slice(b * tokens, (b + 1) * tokens)
            before = stream[l, s, mine, c, b].astype(jnp.float32)
            final[s, b] = (before + update[:, cut]).astype(jnp.bfloat16)

        @pl.when(l + 1 < LAYERS)
        def _():
            stream[1, s, mine, c] = final[s]
            swap_desc(s).start()
            ag_send(t + group, mine)

        @pl.when(l + 1 == LAYERS)
        def _():
            end_desc(s).start()
            out[side * group + s] = final[s, side]

    start_sample(0)
    for k in range(2, CHUNKS):
        bias_chunk(k)
        bias_exchange(0, k)
        bias_pass(0, k - 2)
    stage_first(0, mine)
    bias_pass(0, CHUNKS - 2)
    start_sample(1)
    bias_pass(0, CHUNKS - 1)
    stage_first(0, other)
    for k in range(CHUNKS):
        bias_exchange(1, k)
    settle(mask_buf.at[pl.ds(0, rows - 1)], mask_sems.at[1])
    load(CHUNKS).wait()
    load(CHUNKS + 1).wait()

    forward(0, mine)
    forward(0, other)

    def step(t, carry):
        @pl.when(t < tasks)
        def _():
            project(t)

        @pl.when(t + 1 < group)
        def _():
            stage_first(t + 1, mine)
            stage_first(t + 1, other)

        @pl.when(t + 2 < group)
        def _():
            start_sample(t + 2)

        @pl.when(t == 0)
        def _():
            bias_arrived(0)

        @pl.when(t == group)
        def _():
            bias_arrived(1)

        @pl.when(t < tasks)
        def _():
            attend(t)
            gated_desc(t, 1).start()
            gated_desc(t, 0).start()

        for k in range(CHUNKS):

            @pl.when(t == max(k - 1, 0))
            def _(k=k):
                bias_pass(1, k)

        @pl.when((t >= 1) & (t < tasks))
        def _():
            pass_gated(t - 1)

        @pl.when(t + 1 < tasks - RELAYED)
        def _():
            forward(t + 1, mine)

        @pl.when((t + 2 >= tasks - RELAYED) & (t + 2 < tasks))
        def _():
            forward(t + 2, mine)
            relay_desc(t + 2).start()

        @pl.when((t >= 1) & (t <= group))
        def _():
            finish(t - 1)

        @pl.when(t >= group + 2)
        def _():
            finish(t - 2)

        @pl.when(t + 1 < tasks)
        def _():
            forward(t + 1, other)

        @pl.when((t + 2 >= group) & (t + 2 < tasks))
        def _():
            stage_next(t + 2)

        return carry

    lax.fori_loop(0, tasks + 1, step, 0)
    pass_gated(tasks - 1)
    finish(jnp.int32(tasks - 1))

    settle(out.at[pl.ds((1 - side) * group, group)], end_sems.at[1])
    settle(parts_buf.at[pl.ds(0, cols - 1)], part_sems.at[0])
    settle(mask_buf.at[pl.ds(0, rows - 1)], mask_sems.at[0])
    for l in range(LAYERS):
        settle(spread.at[l, 0, pl.ds(0, cols - 1)], a2a_sems.at[l, CHUNKS])
        settle(spread.at[l, 0], pair_sems.at[0, l])
    settle(stream.at[0, pl.ds(0, group), 0, pl.ds(0, 3), 0], in_sems.at[2, 0])
    settle(stream.at[1, pl.ds(0, group), 0, 0], swap_sems.at[group])
    settle(gated.at[:, :, pl.ds(0, 3)], gated_sems.at[2, 0])
    settle(out.at[pl.ds(0, group)], end_sems.at[0])

    def drain(t, carry):
        settle(stream.at[0, 0, :, pl.ds(0, 3)], ag_sems.at[t, 4])
        return carry

    lax.fori_loop(0, tasks, drain, 0)


def pair_normed(rows_in):
    chans = rows_in.shape[1]
    if chans & (chans - 1):
        return layer_norm(rows_in.astype(jnp.float32)).astype(jnp.bfloat16)
    share = jnp.full((chans, chans), 1.0 / chans, jnp.bfloat16)
    average = jnp.dot(rows_in, share, preferred_element_type=jnp.float32)
    centered = rows_in.astype(jnp.float32) - average
    square = centered * centered
    high = square.astype(jnp.bfloat16)
    low = (square - high.astype(jnp.float32)).astype(jnp.bfloat16)
    variance = jnp.dot(
        jnp.concatenate([high, low], axis=1),
        jnp.concatenate([share, share], axis=0),
        preferred_element_type=jnp.float32,
    )
    return (centered * lax.rsqrt(variance + EPS)).astype(jnp.bfloat16)


def per_device_fused(
    rows,
    cols,
    single,
    pair_act,
    token_mask,
    atom_feats,
    atom_token,
    atom_count,
    atom_weight,
    bias_weight,
    qkvg_weight,
    out_weight,
):
    samples, tokens, width = single.shape
    single = single.transpose(0, 2, 1)
    group = samples // 2
    heads = width // HEAD_DIM
    chans = atom_feats.shape[1]
    slots = atom_feats.shape[0]
    pairs = pair_act.shape[2]
    all_heads = bias_weight.shape[1] * bias_weight.shape[2]
    bf16, f32 = jnp.bfloat16, jnp.float32
    dma = pltpu.SemaphoreType.DMA
    updated = pl.pallas_call(
        lambda *refs: fused(rows, cols, *refs),
        out_shape=jax.ShapeDtypeStruct(single.shape, bf16),
        in_specs=[pl.BlockSpec(memory_space=pl.ANY)]
        + [pl.BlockSpec(memory_space=pltpu.VMEM)] * 7
        + [pl.BlockSpec(memory_space=pl.ANY)] * 2,
        out_specs=pl.BlockSpec(memory_space=pltpu.VMEM),
        scratch_shapes=[
            pltpu.VMEM(pair_act.shape, bf16),
            pltpu.VMEM((LAYERS, cols, heads, tokens, tokens), bf16),
            pltpu.VMEM(qkvg_weight.shape, bf16),
            pltpu.VMEM(out_weight.shape, bf16),
            pltpu.VMEM((LAYERS, 2, cols, heads, tokens, tokens), bf16),
            pltpu.VMEM((LAYERS, group, 2, cols, 2, width, tokens), bf16),
            pltpu.VMEM((samples, width, tokens), bf16),
            pltpu.VMEM((cols, tokens + 16, chans), bf16),
            pltpu.VMEM((width, tokens), f32),
            pltpu.VMEM((rows, 1, tokens), jnp.int32),
            pltpu.VMEM((2 * tokens, width), bf16),
            pltpu.VMEM((2, width, 2 * tokens), bf16),
            pltpu.VMEM((2, width, 2 * tokens), bf16),
            pltpu.VMEM((width, 2 * tokens), f32),
            pltpu.VMEM((LAYERS, group, cols, width, 2 * tokens), bf16),
            pltpu.VMEM((group, 2, width, tokens), bf16),
            dma((2,)),
            dma((2,)),
            dma((LAYERS, CHUNKS + 1)),
            dma((2, LAYERS)),
            dma((3, group)),
            dma((LAYERS * group, 5)),
            dma((group + 1,)),
            dma((3, LAYERS * group)),
            dma((2,)),
            dma((CHUNKS + 2,)),
        ],
        compiler_params=pltpu.CompilerParams(
            collective_id=0, has_side_effects=True, vmem_limit_bytes=56 * 1024 * 1024
        ),
        name="fused_blocks",
    )(
        pair_act,
        bias_weight.reshape(pairs, all_heads).T,
        single,
        atom_feats,
        atom_token.reshape(1, slots),
        atom_count.reshape(1, 1),
        atom_weight.T,
        token_mask.reshape(1, tokens),
        qkvg_weight,
        out_weight,
    )
    return updated.transpose(0, 2, 1)


def solution(mesh):
    rows, cols = mesh.shape["row"], mesh.shape["col"]
    placed = (
        P(None, ("parts", "row"), "col"),
        P(("parts", "row"), "col", None),
        P(("parts", "row")),
        P(("parts", "row", "col"), None),
        P(("parts", "row", "col")),
        P(("parts", "row", "col")),
        P(None, "col"),
        P(),
        P(None, None, "col", None),
        P(None, "col", None),
    )

    def body(single, *rest):
        pairs = rest[0].shape
        square = rows == cols == 4 and single.shape[0] % 4 == 0 and pairs[0] == pairs[1]
        square = square and pairs[0] % 128 == 0
        if square and single.shape[2] % HEAD_DIM == 0:
            return per_device_fused(rows, cols, single, *rest)
        return per_device(single, *rest)

    return jax.shard_map(
        body,
        mesh=mesh,
        in_specs=placed,
        out_specs=P(None, ("parts", "row"), "col"),
        check_vma=False,
    )
```

```python
import math

import jax
import jax.numpy as jnp
from jax import lax
from jax.experimental import pallas as pl
from jax.experimental.pallas import tpu as pltpu
from jax.sharding import PartitionSpec as P

HEAD_DIM = 48
LAYERS = 2
CHUNKS = 4


EPS = 1e-05
MASKED = -1000000000.0
START_LOW = -1e30


def layer_norm(values):
    average = jnp.mean(values, axis=-1, keepdims=True)
    centered = values - average
    variance = jnp.mean(centered * centered, axis=-1, keepdims=True)
    return centered * lax.rsqrt(variance + EPS)


def per_device(
    single,
    pair_act,
    token_mask,
    atom_feats,
    atom_token,
    atom_count,
    atom_weight,
    bias_weight,
    qkvg_weight,
    out_weight,
):
    tok_rows = single.shape[1]
    sample_count = single.shape[0]
    slot_ids = jnp.arange(atom_feats.shape[0], dtype=jnp.int32)
    live_slots = slot_ids < atom_count[0]
    token_ids = jnp.arange(tok_rows, dtype=jnp.int32)
    owner_match = (token_ids[:, None] == atom_token[None, :]) & live_slots[None, :]
    owners = owner_match.astype(jnp.float32)
    counts = jnp.sum(owners, axis=1)
    atom_sums = jnp.dot(
        owner_match.astype(jnp.bfloat16), atom_feats, preferred_element_type=jnp.float32
    )
    sum_total, count_total = (
        lax.psum(atom_sums.astype(jnp.bfloat16), "col").astype(jnp.float32),
        lax.psum(counts[:, None].astype(jnp.bfloat16), "col").astype(jnp.float32),
    )
    pooled = (
        jnp.dot(sum_total, atom_weight.astype(jnp.float32), precision=lax.Precision.HIGHEST)
        / count_total
    )
    stream = (single.astype(jnp.float32) + pooled[None]).astype(jnp.bfloat16)
    pair_normed = layer_norm(pair_act.astype(jnp.float32)).astype(jnp.bfloat16)
    biases = jnp.einsum(
        "ijc,clh->lhij", pair_normed, bias_weight, preferred_element_type=jnp.float32
    ).astype(jnp.bfloat16)
    live_keys = (token_mask > 0).astype(jnp.bfloat16)[None, :]
    score_scale = 1.0 / math.sqrt(HEAD_DIM)
    for layer_idx in range(LAYERS):
        spread = lax.all_to_all(biases[layer_idx], "col", split_axis=0, concat_axis=2, tiled=True)
        gathered = lax.all_gather(stream, "col", axis=2, tiled=True)
        normed = layer_norm(gathered.astype(jnp.float32)).astype(jnp.bfloat16)
        projected = jnp.einsum(
            "std,fed->fste", normed, qkvg_weight[layer_idx], preferred_element_type=jnp.float32
        )
        head_width = projected.shape[3]
        heads_here = head_width // HEAD_DIM
        queries = (
            projected[0].astype(jnp.bfloat16).reshape(sample_count, tok_rows, heads_here, HEAD_DIM)
        )
        key_rows = projected[1].astype(jnp.bfloat16)
        value_rows = projected[2].astype(jnp.bfloat16)
        gating = jax.nn.sigmoid(projected[3])

        def attend(running, incoming, offset, queries=queries, spread=spread):
            top_old, summed_old, acc_old = running
            keys_in, values_in, live_in = incoming
            key_count = keys_in.shape[1]
            keys_heads = keys_in.reshape(sample_count, key_count, heads_here, HEAD_DIM)
            values_heads = values_in.reshape(sample_count, key_count, heads_here, HEAD_DIM)
            scores = (
                jnp.einsum(
                    "sqhd,skhd->shqk", queries, keys_heads, preferred_element_type=jnp.float32
                )
                * score_scale
            )
            scores = scores + spread.astype(jnp.float32)[None]
            scores = jnp.where(live_in[0][None, None, None, :] > 0, scores, MASKED)
            top_new = jnp.maximum(top_old, jnp.max(scores, axis=-1))
            exponent = jnp.exp(scores - top_new[..., None])
            summed_new = jnp.sum(exponent, axis=-1)
            weights = exponent.astype(jnp.bfloat16)
            acc_new = jnp.einsum(
                "shqk,skhd->shqd", weights, values_heads, preferred_element_type=jnp.float32
            )
            return (top_new, summed_new, acc_new)

        start_state = (
            jnp.full((sample_count, heads_here, tok_rows), START_LOW, jnp.float32),
            jnp.zeros((sample_count, heads_here, tok_rows), jnp.float32),
            jnp.zeros((sample_count, heads_here, tok_rows, HEAD_DIM), jnp.float32),
        )
        top_end, summed_end, acc_end = attend(
            start_state,
            (
                lax.all_gather(key_rows, "row", axis=1, tiled=True),
                lax.all_gather(value_rows, "row", axis=1, tiled=True),
                lax.all_gather(live_keys, "row", axis=1, tiled=True),
            ),
            jnp.int32(0),
        )
        attended = acc_end / summed_end[..., None]
        attended = attended.transpose(0, 2, 1, 3).reshape(sample_count, tok_rows, head_width)
        gated = (gating * attended).astype(jnp.bfloat16)
        out_rows = out_weight[layer_idx]

        def project(summed, incoming, offset, out_rows=out_rows):
            return jnp.einsum("std,ed->ste", incoming, out_rows, preferred_element_type=jnp.float32)

        zero_update = jnp.zeros((sample_count, tok_rows, out_rows.shape[0]), jnp.float32)
        update = project(
            zero_update, lax.all_gather(gated, "col", axis=2, tiled=True), jnp.int32(0)
        )
        stream = (stream.astype(jnp.float32) + update).astype(jnp.bfloat16)
    return stream


MESH = pl.DeviceIdType.MESH
NT = (((1,), (1,)), ((), ()))


def remote(src, dst, send_sem, recv_sem, row, col):
    return pltpu.make_async_remote_copy(
        src_ref=src,
        dst_ref=dst,
        send_sem=send_sem,
        recv_sem=recv_sem,
        device_id={"row": row, "col": col},
        device_id_type=MESH,
    )


def fused(
    rows,
    cols,
    pair_hbm,
    bias_w_hbm,
    single_hbm,
    feats_hbm,
    slot_token_hbm,
    slot_count_hbm,
    atom_weight_hbm,
    mask_hbm,
    qkvg_hbm,
    out_w_hbm,
    out,
    pair,
    bias_w,
    single,
    feats,
    slot_token,
    slot_count,
    atom_weight,
    mask,
    qkvg,
    out_w,
    bias,
    spread,
    stream,
    first,
    parts_buf,
    pooled,
    mask_buf,
    queries,
    keys,
    values,
    gates,
    gated,
    final,
    part_sems,
    mask_sems,
    a2a_sems,
    pair_sems,
    in_sems,
    ag_sems,
    swap_sems,
    gated_sems,
    end_sems,
    load_sems,
):
    r = lax.axis_index("row")
    c = lax.axis_index("col")
    samples, width, tokens = single.shape
    group = samples // 2
    tasks = LAYERS * group
    full = width * cols
    heads = width // HEAD_DIM
    sibling = c + 1 - 2 * lax.rem(c, 2)
    across = lax.rem(c + 2, cols)
    side = lax.rem(r, 2)
    mine = lax.div(r, 2)
    other = 1 - mine
    near = r + 1 - 2 * side
    peer_rows = {1: near, 2: lax.rem(r + 2, rows), 3: lax.rem(near + 2, rows)}

    lines = tokens // CHUNKS

    small = (
        (feats_hbm, feats),
        (slot_token_hbm, slot_token),
        (slot_count_hbm, slot_count),
        (bias_w_hbm, bias_w),
        (mask_hbm, mask),
        (atom_weight_hbm, atom_weight),
        (single_hbm, single),
        (qkvg_hbm, qkvg),
        (out_w_hbm, out_w),
    )

    def load(k):
        if k < CHUNKS:
            at = pl.ds(k * lines, lines)
            return pltpu.make_async_copy(pair_hbm.at[at], pair.at[at], load_sems.at[k])
        src, dst = small[k - CHUNKS]
        return pltpu.make_async_copy(src, dst, load_sems.at[k])

    for k in (0, *range(CHUNKS, CHUNKS + 5), *range(1, CHUNKS), *range(CHUNKS + 5, CHUNKS + 9)):
        load(k).start()

    barrier = pltpu.get_barrier_semaphore()
    for dc in range(1, cols):
        pl.semaphore_signal(
            barrier,
            inc=1,
            device_id={"row": r, "col": lax.rem(c + dc, cols)},
            device_id_type=MESH,
        )
    for d in range(1, rows):
        pl.semaphore_signal(
            barrier, inc=1, device_id={"row": peer_rows[d], "col": c}, device_id_type=MESH
        )
    def col_of(d):
        return lax.rem(c + d, cols)

    def rows_at(k):
        return pl.ds(k * lines, lines)

    def bias_chunk(k):
        load(k).wait()
        here = pair_normed(pair[rows_at(k)].reshape(lines * tokens, pair.shape[2]))
        made = lax.dot_general(bias_w[...], here, NT, preferred_element_type=jnp.float32)
        made = made.astype(jnp.bfloat16).reshape(LAYERS, cols, heads, lines, tokens)
        bias[:, :, :, rows_at(k)] = made

    def settle(ref, sem):
        pltpu.make_async_copy(ref, ref, sem).wait()

    def a2a_desc(l, d, k):
        to = col_of(d)
        return remote(
            bias.at[l, to, :, rows_at(k)],
            spread.at[l, side, c, :, rows_at(k)],
            a2a_sems.at[l, CHUNKS],
            a2a_sems.at[l, k],
            r,
            to,
        )

    def pair_desc(l, d, k):
        block = col_of(cols - d) if d else c
        held = spread.at[l, side, block, :, rows_at(k)]
        return remote(
            held if d else bias.at[l, c, :, rows_at(k)],
            held,
            pair_sems.at[0, l],
            pair_sems.at[1, l],
            near,
            c,
        )

    def bias_exchange(l, k):
        for d in (2, 3, 1):
            a2a_desc(l, d, k).start()
        if l == 0:
            pair_desc(l, 0, k).start()
        spread[l, side, c, :, rows_at(k)] = bias[l, c, :, rows_at(k)]

    def bias_pass(l, k):
        if l:
            pair_desc(l, 0, k).start()
        settle(spread.at[l, side, pl.ds(0, cols - 1), :, rows_at(k)], a2a_sems.at[l, k])
        for d in range(1, cols):
            pair_desc(l, d, k).start()

    def bias_arrived(l):
        settle(spread.at[l, 1 - side], pair_sems.at[1, l])

    slots = feats.shape[0]
    for k in range(5):
        load(CHUNKS + k).wait()
    token_ids = lax.broadcasted_iota(jnp.int32, (tokens, slots), 0)
    slot_ids = lax.broadcasted_iota(jnp.int32, (tokens, slots), 1)
    match = (token_ids == slot_token[...]) & (slot_ids < slot_count[...])
    owners = jnp.where(match, 1.0, 0.0).astype(jnp.bfloat16)
    parts_buf[c, 0:tokens] = jnp.dot(
        owners, feats[...], preferred_element_type=jnp.float32
    ).astype(jnp.bfloat16)
    parts_buf[c, tokens : tokens + 16] = lax.dot_general(
        jnp.ones((16, slots), jnp.bfloat16), owners, NT, preferred_element_type=jnp.float32
    ).astype(jnp.bfloat16)
    bias_chunk(0)
    pl.semaphore_wait(barrier, cols - 1 + rows - 1)
    for d in range(1, cols):
        remote(
            parts_buf.at[c], parts_buf.at[c], part_sems.at[0], part_sems.at[1], r, col_of(d)
        ).start()
    for d in range(1, rows):
        remote(mask, mask_buf.at[r], mask_sems.at[0], mask_sems.at[1], peer_rows[d], c).start()
    mask_buf[r] = mask[...]

    bias_exchange(0, 0)
    bias_chunk(1)
    bias_exchange(0, 1)
    settle(parts_buf.at[pl.ds(0, cols - 1)], part_sems.at[1])
    load(CHUNKS + 5).wait()
    load(CHUNKS + 6).wait()
    total = jnp.zeros((width, tokens), jnp.float32)
    count_row = jnp.zeros((1, tokens), jnp.float32)
    for k in range(cols):
        total = total + lax.dot_general(
            atom_weight[...], parts_buf[k, 0:tokens], NT, preferred_element_type=jnp.float32
        )
        count_row = count_row + parts_buf[k, tokens : tokens + 16].astype(jnp.float32)[0:1]
    pooled[...] = total / count_row

    def in_desc(d, s):
        at = s + group * (side if d == 2 else 1 - side)
        return remote(
            first.at[at],
            stream.at[0, s, mine, c, side],
            in_sems.at[2, 0],
            in_sems.at[min(d, 2) - 1, s],
            peer_rows[d],
            c,
        )

    def start_sample(s):
        for k in range(2):
            at = s + group * k
            first[at] = (single[at].astype(jnp.float32) + pooled[...]).astype(jnp.bfloat16)
        stream[0, s, mine, c, side] = first[s + group * side]
        for d in (1, 2, 3):
            in_desc(d, s).start()

    def ag_desc(t, half, kind):
        l, s = lax.div(t, group), lax.rem(t, group)
        block = across if kind == 2 else c
        return remote(
            stream.at[l, s, half, block],
            stream.at[l, s, half, block],
            ag_sems.at[t, 4],
            ag_sems.at[t, 2 * half + kind % 2],
            r,
            across if kind == 1 else sibling,
        )

    def ag_arrived(t, half, kind):
        l, s = lax.div(t, group), lax.rem(t, group)
        held = stream.at[l, s, half, across] if kind else stream.at[l, s, half, pl.ds(0, 2)]
        settle(held, ag_sems.at[t, 2 * half + kind])

    def ag_send(t, half):
        ag_desc(t, half, 1).start()
        ag_desc(t, half, 0).start()

    def swap_desc(s):
        return remote(
            stream.at[1, s, mine, c],
            stream.at[1, s, mine, c],
            swap_sems.at[group],
            swap_sems.at[s],
            peer_rows[2],
            c,
        )

    def stage_first(t, half):
        if half is mine:
            settle(first.at[0], in_sems.at[0, t])
        else:
            settle(stream.at[0, t, other, c], in_sems.at[1, t])
        ag_send(t, half)

    def stage_next(t):
        s = lax.rem(t, group)
        settle(stream.at[1, s, other, c], swap_sems.at[s])
        ag_send(t, other)

    def forward(t, half):
        ag_arrived(t, half, 1)
        ag_desc(t, half, 2).start()

    score_scale = 1.0 / math.sqrt(HEAD_DIM)

    def normed_half(l, s, half):
        here = jnp.concatenate(
            [
                jnp.concatenate([stream[l, s, half, k, b] for k in range(cols)], axis=0)
                for b in range(2)
            ],
            axis=1,
        ).astype(jnp.float32)
        average = jnp.mean(here, axis=0, keepdims=True)
        centered = here - average
        variance = jnp.mean(centered * centered, axis=0, keepdims=True)
        return (centered * lax.rsqrt(variance + EPS)).astype(jnp.bfloat16)

    def project(t):
        l, s = lax.div(t, group), lax.rem(t, group)
        for half in (mine, other):
            ag_arrived(t, half, 0)
            here = normed_half(l, s, half)

            def rows_of(f, here=here):
                return jnp.dot(qkvg[l, f], here, preferred_element_type=jnp.float32)

            keys[half] = rows_of(1).astype(jnp.bfloat16)
            values[half] = rows_of(2).astype(jnp.bfloat16)
            if half is mine:
                query, gating = rows_of(0).T.astype(jnp.bfloat16), jax.nn.sigmoid(rows_of(3))
                for b in range(2):
                    queries[b] = query[b * tokens : (b + 1) * tokens]
                    gates[b] = gating[:, b * tokens : (b + 1) * tokens]

    def attend(t, last=False):
        l, s = lax.div(t, group), lax.rem(t, group)
        live = jnp.concatenate([mask_buf[k] for k in range(rows)], axis=1) > 0
        square = lax.broadcasted_iota(jnp.int32, (tokens, tokens), 0) == lax.broadcasted_iota(
            jnp.int32, (tokens, tokens), 1
        )

        def one(h, b):
            at = slice(h * HEAD_DIM, (h + 1) * HEAD_DIM)
            key_here = jnp.concatenate([keys[k, at] for k in range(2)], axis=1)
            value_here = jnp.concatenate([values[k, at] for k in range(2)], axis=1)
            scores = (
                jnp.dot(queries[b, :, at], key_here, preferred_element_type=jnp.float32)
                * score_scale
            )
            head_bias = jnp.concatenate([spread[l, b, k, h] for k in range(cols)], axis=1)
            scores = scores + head_bias.astype(jnp.float32)
            scores = jnp.where(live, scores, MASKED)
            highest = jnp.max(scores, axis=-1, keepdims=True)
            exponent = jnp.exp(scores - highest)
            summed = jnp.sum(exponent, axis=-1, keepdims=True)
            mixed = lax.dot_general(
                value_here,
                exponent.astype(jnp.bfloat16),
                NT,
                preferred_element_type=jnp.float32,
            )
            summed_row = jnp.sum(jnp.where(square, summed, 0.0), axis=0, keepdims=True)
            attended = mixed * (1.0 / summed_row)
            gated[l, s, b, c, at] = (gates[b, at] * attended).astype(jnp.bfloat16)

        if last:
            for b in (1 - side, side):
                for h in range(heads):
                    one(h, b)
                gated_desc(t, 1, b).start()
                gated_desc(t, 0, b).start()
        else:
            for h in range(heads):
                for b in range(2):
                    one(h, b)
            gated_desc(t, 1).start()
            gated_desc(t, 0).start()

    def gated_desc(t, kind, b=None):
        l, s = lax.div(t, group), lax.rem(t, group)
        block = across if kind == 2 else c
        held = gated.at[l, s, :, block] if b is None else gated.at[l, s, b, block]
        return remote(
            held,
            held,
            gated_sems.at[2, 0, 0],
            gated_sems.at[kind % 2, 0 if b is None else b, t],
            r,
            across if kind == 1 else sibling,
        )

    def end_desc(s):
        return remote(
            final.at[s, 1 - side],
            out.at[side * group + s],
            end_sems.at[0],
            end_sems.at[1],
            near,
            c,
        )

    def pass_gated(t):
        l, s = lax.div(t, group), lax.rem(t, group)
        settle(gated.at[l, s, :, across], gated_sems.at[1, 0, t])
        gated_desc(t, 2).start()

    def pass_last(t, b):
        l, s = LAYERS - 1, lax.rem(t, group)
        settle(gated.at[l, s, b, across], gated_sems.at[1, b, t])
        gated_desc(t, 2, b).start()

    def finish_last(t, b):
        l, s = LAYERS - 1, lax.rem(t, group)
        settle(gated.at[l, s, b, pl.ds(0, 2)], gated_sems.at[0, b, t])
        joined = jnp.concatenate([gated[l, s, b, k] for k in range(cols)], axis=0)
        update = jnp.dot(out_w[l], joined, preferred_element_type=jnp.float32)
        return (stream[l, s, mine, c, b].astype(jnp.float32) + update).astype(jnp.bfloat16)

    def finish(t):
        l, s = lax.div(t, group), lax.rem(t, group)
        settle(gated.at[l, s, :, pl.ds(0, 2)], gated_sems.at[0, 0, t])
        joined = jnp.concatenate(
            [
                jnp.concatenate([gated[l, s, b, k] for k in range(cols)], axis=0)
                for b in range(2)
            ],
            axis=1,
        )
        update = jnp.dot(out_w[l], joined, preferred_element_type=jnp.float32)
        for b in range(2):
            cut = slice(b * tokens, (b + 1) * tokens)
            before = stream[l, s, mine, c, b].astype(jnp.float32)
            final[s, b] = (before + update[:, cut]).astype(jnp.bfloat16)

        @pl.when(l + 1 < LAYERS)
        def _():
            stream[1, s, mine, c] = final[s]
            swap_desc(s).start()
            ag_send(t + group, mine)

        @pl.when(l + 1 == LAYERS)
        def _():
            end_desc(s).start()
            out[side * group + s] = final[s, side]

    start_sample(0)
    for k in range(2, CHUNKS):
        bias_chunk(k)
        bias_exchange(0, k)
        bias_pass(0, k - 2)
        if k == 2:
            start_sample(1)
    stage_first(0, mine)
    bias_pass(0, CHUNKS - 2)
    stage_first(0, other)
    bias_pass(0, CHUNKS - 1)
    start_sample(2)
    stage_first(1, mine)
    forward(0, mine)
    stage_first(1, other)
    for k in range(CHUNKS):
        bias_exchange(1, k)
    settle(mask_buf.at[pl.ds(0, rows - 1)], mask_sems.at[1])
    load(CHUNKS + 7).wait()
    load(CHUNKS + 8).wait()

    forward(0, other)

    def step(t, carry):
        project(t)

        for k in range(CHUNKS):

            @pl.when(t == max(k, 1))
            def _(k=k):
                bias_pass(1, k)

        @pl.when(t == 0)
        def _():
            bias_arrived(0)

        @pl.when(t == group)
        def _():
            bias_arrived(1)

        @pl.when(t == 0)
        def _():
            for s in range(3, group):
                start_sample(s)

        attend(t)

        @pl.when(t >= 1)
        def _():
            pass_gated(t - 1)

        @pl.when(t + 2 < group)
        def _():
            stage_first(t + 2, mine)
            stage_first(t + 2, other)

        forward(t + 1, mine)

        @pl.when((t >= 1) & (t <= group))
        def _():
            finish(t - 1)

        @pl.when(t >= group + 2)
        def _():
            finish(t - 2)

        @pl.when((t + 2 >= group) & (t + 2 < tasks))
        def _():
            stage_next(t + 2)

        forward(t + 1, other)

        return carry

    lax.fori_loop(0, tasks - 1, step, 0)
    final_task = jnp.int32(tasks - 1)
    project(final_task)
    attend(final_task, True)
    pass_gated(final_task - 1)
    for k in (2, 1):
        finish(final_task - k)
    for b in (1 - side, side):
        pass_last(final_task, b)
    final[group - 1, 1 - side] = finish_last(final_task, 1 - side)
    end_desc(group - 1).start()
    out[side * group + group - 1] = finish_last(final_task, side)

    settle(out.at[pl.ds((1 - side) * group, group)], end_sems.at[1])
    settle(parts_buf.at[pl.ds(0, cols - 1)], part_sems.at[0])
    settle(mask_buf.at[pl.ds(0, rows - 1)], mask_sems.at[0])
    for l in range(LAYERS):
        settle(spread.at[l, 0, pl.ds(0, cols - 1)], a2a_sems.at[l, CHUNKS])
        settle(spread.at[l, 0], pair_sems.at[0, l])
    settle(stream.at[0, pl.ds(0, group), 0, pl.ds(0, 3), 0], in_sems.at[2, 0])
    settle(stream.at[1, pl.ds(0, group), 0, 0], swap_sems.at[group])
    settle(gated.at[:, :, :, pl.ds(0, 3)], gated_sems.at[2, 0, 0])
    settle(out.at[pl.ds(0, group)], end_sems.at[0])

    def drain(t, carry):
        settle(stream.at[0, 0, :, pl.ds(0, 3)], ag_sems.at[t, 4])
        return carry

    lax.fori_loop(0, tasks, drain, 0)


def pair_normed(rows_in):
    chans = rows_in.shape[1]
    if chans & (chans - 1):
        return layer_norm(rows_in.astype(jnp.float32)).astype(jnp.bfloat16)
    share = jnp.full((chans, chans), 1.0 / chans, jnp.bfloat16)
    average = jnp.dot(rows_in, share, preferred_element_type=jnp.float32)
    centered = rows_in.astype(jnp.float32) - average
    square = centered * centered
    variance = jnp.dot(square.astype(jnp.bfloat16), share, preferred_element_type=jnp.float32)
    return (centered * lax.rsqrt(variance + EPS)).astype(jnp.bfloat16)


def per_device_fused(
    rows,
    cols,
    single,
    pair_act,
    token_mask,
    atom_feats,
    atom_token,
    atom_count,
    atom_weight,
    bias_weight,
    qkvg_weight,
    out_weight,
):
    samples, tokens, width = single.shape
    single = single.transpose(0, 2, 1)
    group = samples // 2
    heads = width // HEAD_DIM
    chans = atom_feats.shape[1]
    slots = atom_feats.shape[0]
    pairs = pair_act.shape[2]
    all_heads = bias_weight.shape[1] * bias_weight.shape[2]
    bf16, f32 = jnp.bfloat16, jnp.float32
    dma = pltpu.SemaphoreType.DMA
    updated = pl.pallas_call(
        lambda *refs: fused(rows, cols, *refs),
        out_shape=jax.ShapeDtypeStruct(single.shape, bf16),
        in_specs=[pl.BlockSpec(memory_space=pl.ANY)] * 10,
        out_specs=pl.BlockSpec(memory_space=pltpu.VMEM),
        scratch_shapes=[
            pltpu.VMEM(pair_act.shape, bf16),
            pltpu.VMEM((all_heads, pairs), bf16),
            pltpu.VMEM(single.shape, bf16),
            pltpu.VMEM(atom_feats.shape, bf16),
            pltpu.VMEM((1, slots), jnp.int32),
            pltpu.VMEM((1, 1), jnp.int32),
            pltpu.VMEM((width, chans), bf16),
            pltpu.VMEM((1, tokens), jnp.int32),
            pltpu.VMEM(qkvg_weight.shape, bf16),
            pltpu.VMEM(out_weight.shape, bf16),
            pltpu.VMEM((LAYERS, cols, heads, tokens, tokens), bf16),
            pltpu.VMEM((LAYERS, 2, cols, heads, tokens, tokens), bf16),
            pltpu.VMEM((LAYERS, group, 2, cols, 2, width, tokens), bf16),
            pltpu.VMEM((samples, width, tokens), bf16),
            pltpu.VMEM((cols, tokens + 16, chans), bf16),
            pltpu.VMEM((width, tokens), f32),
            pltpu.VMEM((rows, 1, tokens), jnp.int32),
            pltpu.VMEM((2, tokens, width), bf16),
            pltpu.VMEM((2, width, 2 * tokens), bf16),
            pltpu.VMEM((2, width, 2 * tokens), bf16),
            pltpu.VMEM((2, width, tokens), f32),
            pltpu.VMEM((LAYERS, group, 2, cols, width, tokens), bf16),
            pltpu.VMEM((group, 2, width, tokens), bf16),
            dma((2,)),
            dma((2,)),
            dma((LAYERS, CHUNKS + 1)),
            dma((2, LAYERS)),
            dma((3, group)),
            dma((LAYERS * group, 5)),
            dma((group + 1,)),
            dma((3, 2, LAYERS * group)),
            dma((2,)),
            dma((CHUNKS + 9,)),
        ],
        compiler_params=pltpu.CompilerParams(
            collective_id=0, has_side_effects=True, vmem_limit_bytes=56 * 1024 * 1024
        ),
        name="fused_blocks",
    )(
        pair_act,
        bias_weight.reshape(pairs, all_heads).T,
        single,
        atom_feats,
        atom_token.reshape(1, slots),
        atom_count.reshape(1, 1),
        atom_weight.T,
        token_mask.reshape(1, tokens),
        qkvg_weight,
        out_weight,
    )
    return updated.transpose(0, 2, 1)


def solution(mesh):
    rows, cols = mesh.shape["row"], mesh.shape["col"]
    placed = (
        P(None, ("parts", "row"), "col"),
        P(("parts", "row"), "col", None),
        P(("parts", "row")),
        P(("parts", "row", "col"), None),
        P(("parts", "row", "col")),
        P(("parts", "row", "col")),
        P(None, "col"),
        P(),
        P(None, None, "col", None),
        P(None, "col", None),
    )

    def body(single, *rest):
        pairs = rest[0].shape
        square = rows == cols == 4 and single.shape[0] % 4 == 0 and pairs[0] == pairs[1]
        square = square and pairs[0] % 128 == 0
        if square and single.shape[2] % HEAD_DIM == 0:
            return per_device_fused(rows, cols, single, *rest)
        return per_device(single, *rest)

    return jax.shard_map(
        body,
        mesh=mesh,
        in_specs=placed,
        out_specs=P(None, ("parts", "row"), "col"),
        check_vma=False,
    )
```

```python
import math

import jax
import jax.numpy as jnp
from jax import lax
from jax.experimental import pallas as pl
from jax.experimental.pallas import tpu as pltpu
from jax.sharding import PartitionSpec as P

HEAD_DIM = 48
LAYERS = 2
CHUNKS = 4


EPS = 1e-05
MASKED = -1000000000.0
START_LOW = -1e30


def layer_norm(values):
    average = jnp.mean(values, axis=-1, keepdims=True)
    centered = values - average
    variance = jnp.mean(centered * centered, axis=-1, keepdims=True)
    return centered * lax.rsqrt(variance + EPS)


def per_device(
    single,
    pair_act,
    token_mask,
    atom_feats,
    atom_token,
    atom_count,
    atom_weight,
    bias_weight,
    qkvg_weight,
    out_weight,
):
    tok_rows = single.shape[1]
    sample_count = single.shape[0]
    slot_ids = jnp.arange(atom_feats.shape[0], dtype=jnp.int32)
    live_slots = slot_ids < atom_count[0]
    token_ids = jnp.arange(tok_rows, dtype=jnp.int32)
    owner_match = (token_ids[:, None] == atom_token[None, :]) & live_slots[None, :]
    owners = owner_match.astype(jnp.float32)
    counts = jnp.sum(owners, axis=1)
    atom_sums = jnp.dot(
        owner_match.astype(jnp.bfloat16), atom_feats, preferred_element_type=jnp.float32
    )
    sum_total, count_total = (
        lax.psum(atom_sums.astype(jnp.bfloat16), "col").astype(jnp.float32),
        lax.psum(counts[:, None].astype(jnp.bfloat16), "col").astype(jnp.float32),
    )
    pooled = (
        jnp.dot(sum_total, atom_weight.astype(jnp.float32), precision=lax.Precision.HIGHEST)
        / count_total
    )
    stream = (single.astype(jnp.float32) + pooled[None]).astype(jnp.bfloat16)
    pair_normed = layer_norm(pair_act.astype(jnp.float32)).astype(jnp.bfloat16)
    biases = jnp.einsum(
        "ijc,clh->lhij", pair_normed, bias_weight, preferred_element_type=jnp.float32
    ).astype(jnp.bfloat16)
    live_keys = (token_mask > 0).astype(jnp.bfloat16)[None, :]
    score_scale = 1.0 / math.sqrt(HEAD_DIM)
    for layer_idx in range(LAYERS):
        spread = lax.all_to_all(biases[layer_idx], "col", split_axis=0, concat_axis=2, tiled=True)
        gathered = lax.all_gather(stream, "col", axis=2, tiled=True)
        normed = layer_norm(gathered.astype(jnp.float32)).astype(jnp.bfloat16)
        projected = jnp.einsum(
            "std,fed->fste", normed, qkvg_weight[layer_idx], preferred_element_type=jnp.float32
        )
        head_width = projected.shape[3]
        heads_here = head_width // HEAD_DIM
        queries = (
            projected[0].astype(jnp.bfloat16).reshape(sample_count, tok_rows, heads_here, HEAD_DIM)
        )
        key_rows = projected[1].astype(jnp.bfloat16)
        value_rows = projected[2].astype(jnp.bfloat16)
        gating = jax.nn.sigmoid(projected[3])

        def attend(running, incoming, offset, queries=queries, spread=spread):
            top_old, summed_old, acc_old = running
            keys_in, values_in, live_in = incoming
            key_count = keys_in.shape[1]
            keys_heads = keys_in.reshape(sample_count, key_count, heads_here, HEAD_DIM)
            values_heads = values_in.reshape(sample_count, key_count, heads_here, HEAD_DIM)
            scores = (
                jnp.einsum(
                    "sqhd,skhd->shqk", queries, keys_heads, preferred_element_type=jnp.float32
                )
                * score_scale
            )
            scores = scores + spread.astype(jnp.float32)[None]
            scores = jnp.where(live_in[0][None, None, None, :] > 0, scores, MASKED)
            top_new = jnp.maximum(top_old, jnp.max(scores, axis=-1))
            exponent = jnp.exp(scores - top_new[..., None])
            summed_new = jnp.sum(exponent, axis=-1)
            weights = exponent.astype(jnp.bfloat16)
            acc_new = jnp.einsum(
                "shqk,skhd->shqd", weights, values_heads, preferred_element_type=jnp.float32
            )
            return (top_new, summed_new, acc_new)

        start_state = (
            jnp.full((sample_count, heads_here, tok_rows), START_LOW, jnp.float32),
            jnp.zeros((sample_count, heads_here, tok_rows), jnp.float32),
            jnp.zeros((sample_count, heads_here, tok_rows, HEAD_DIM), jnp.float32),
        )
        top_end, summed_end, acc_end = attend(
            start_state,
            (
                lax.all_gather(key_rows, "row", axis=1, tiled=True),
                lax.all_gather(value_rows, "row", axis=1, tiled=True),
                lax.all_gather(live_keys, "row", axis=1, tiled=True),
            ),
            jnp.int32(0),
        )
        attended = acc_end / summed_end[..., None]
        attended = attended.transpose(0, 2, 1, 3).reshape(sample_count, tok_rows, head_width)
        gated = (gating * attended).astype(jnp.bfloat16)
        out_rows = out_weight[layer_idx]

        def project(summed, incoming, offset, out_rows=out_rows):
            return jnp.einsum("std,ed->ste", incoming, out_rows, preferred_element_type=jnp.float32)

        zero_update = jnp.zeros((sample_count, tok_rows, out_rows.shape[0]), jnp.float32)
        update = project(
            zero_update, lax.all_gather(gated, "col", axis=2, tiled=True), jnp.int32(0)
        )
        stream = (stream.astype(jnp.float32) + update).astype(jnp.bfloat16)
    return stream


MESH = pl.DeviceIdType.MESH
NT = (((1,), (1,)), ((), ()))


def remote(src, dst, send_sem, recv_sem, row, col):
    return pltpu.make_async_remote_copy(
        src_ref=src,
        dst_ref=dst,
        send_sem=send_sem,
        recv_sem=recv_sem,
        device_id={"row": row, "col": col},
        device_id_type=MESH,
    )


def fused(
    rows,
    cols,
    pair_hbm,
    bias_w_hbm,
    single_hbm,
    feats_hbm,
    slot_token_hbm,
    slot_count_hbm,
    atom_weight_hbm,
    mask_hbm,
    qkvg_hbm,
    out_w_hbm,
    out,
    pair,
    bias_w,
    single,
    feats,
    slot_token,
    slot_count,
    atom_weight,
    mask,
    qkvg,
    out_w,
    bias,
    spread,
    stream,
    first,
    parts_buf,
    pooled,
    mask_buf,
    queries,
    keys,
    values,
    gates,
    gated,
    final,
    part_sems,
    mask_sems,
    a2a_sems,
    pair_sems,
    in_sems,
    ag_sems,
    swap_sems,
    gated_sems,
    end_sems,
    load_sems,
):
    r = lax.axis_index("row")
    c = lax.axis_index("col")
    samples, width, tokens = single.shape
    group = samples // 2
    tasks = LAYERS * group
    full = width * cols
    heads = width // HEAD_DIM
    sibling = c + 1 - 2 * lax.rem(c, 2)
    across = lax.rem(c + 2, cols)
    side = lax.rem(r, 2)
    mine = lax.div(r, 2)
    other = 1 - mine
    near = r + 1 - 2 * side
    peer_rows = {1: near, 2: lax.rem(r + 2, rows), 3: lax.rem(near + 2, rows)}

    lines = tokens // CHUNKS

    small = (
        (feats_hbm, feats),
        (slot_token_hbm, slot_token),
        (slot_count_hbm, slot_count),
        (bias_w_hbm, bias_w),
        (mask_hbm, mask),
        (atom_weight_hbm, atom_weight),
        (single_hbm, single),
        (qkvg_hbm, qkvg),
        (out_w_hbm, out_w),
    )

    def load(k):
        if k < CHUNKS:
            at = pl.ds(k * lines, lines)
            return pltpu.make_async_copy(pair_hbm.at[at], pair.at[at], load_sems.at[k])
        src, dst = small[k - CHUNKS]
        return pltpu.make_async_copy(src, dst, load_sems.at[k])

    for k in (0, *range(CHUNKS, CHUNKS + 5), *range(1, CHUNKS), *range(CHUNKS + 5, CHUNKS + 9)):
        load(k).start()

    barrier = pltpu.get_barrier_semaphore()
    for dc in range(1, cols):
        pl.semaphore_signal(
            barrier,
            inc=1,
            device_id={"row": r, "col": lax.rem(c + dc, cols)},
            device_id_type=MESH,
        )
    for d in range(1, rows):
        pl.semaphore_signal(
            barrier, inc=1, device_id={"row": peer_rows[d], "col": c}, device_id_type=MESH
        )
    def col_of(d):
        return lax.rem(c + d, cols)

    def rows_at(k):
        return pl.ds(k * lines, lines)

    def bias_chunk(k):
        load(k).wait()
        here = pair_normed(pair[rows_at(k)].reshape(lines * tokens, pair.shape[2]))
        made = lax.dot_general(bias_w[...], here, NT, preferred_element_type=jnp.float32)
        made = made.astype(jnp.bfloat16).reshape(LAYERS, cols, heads, lines, tokens)
        bias[:, :, :, rows_at(k)] = made

    def settle(ref, sem):
        pltpu.make_async_copy(ref, ref, sem).wait()

    def a2a_desc(l, d, k):
        to = col_of(d)
        return remote(
            bias.at[l, to, :, rows_at(k)],
            spread.at[l, side, c, :, rows_at(k)],
            a2a_sems.at[l, CHUNKS],
            a2a_sems.at[l, k],
            r,
            to,
        )

    def pair_desc(l, d, k):
        block = col_of(cols - d) if d else c
        held = spread.at[l, side, block, :, rows_at(k)]
        return remote(
            held if d else bias.at[l, c, :, rows_at(k)],
            held,
            pair_sems.at[0, l],
            pair_sems.at[1, l],
            near,
            c,
        )

    def bias_exchange(l, k):
        for d in (2, 3, 1):
            a2a_desc(l, d, k).start()
        if l == 0:
            pair_desc(l, 0, k).start()
        spread[l, side, c, :, rows_at(k)] = bias[l, c, :, rows_at(k)]

    def bias_pass(l, k):
        if l:
            pair_desc(l, 0, k).start()
        settle(spread.at[l, side, pl.ds(0, cols - 1), :, rows_at(k)], a2a_sems.at[l, k])
        for d in range(1, cols):
            pair_desc(l, d, k).start()

    def bias_arrived(l):
        settle(spread.at[l, 1 - side], pair_sems.at[1, l])

    slots = feats.shape[0]
    for k in range(5):
        load(CHUNKS + k).wait()
    token_ids = lax.broadcasted_iota(jnp.int32, (tokens, slots), 0)
    slot_ids = lax.broadcasted_iota(jnp.int32, (tokens, slots), 1)
    match = (token_ids == slot_token[...]) & (slot_ids < slot_count[...])
    owners = jnp.where(match, 1.0, 0.0).astype(jnp.bfloat16)
    parts_buf[c, 0:tokens] = jnp.dot(
        owners, feats[...], preferred_element_type=jnp.float32
    ).astype(jnp.bfloat16)
    parts_buf[c, tokens : tokens + 16] = lax.dot_general(
        jnp.ones((16, slots), jnp.bfloat16), owners, NT, preferred_element_type=jnp.float32
    ).astype(jnp.bfloat16)
    bias_chunk(0)
    pl.semaphore_wait(barrier, cols - 1 + rows - 1)
    for d in range(1, cols):
        remote(
            parts_buf.at[c], parts_buf.at[c], part_sems.at[0], part_sems.at[1], r, col_of(d)
        ).start()
    for d in range(1, rows):
        remote(mask, mask_buf.at[r], mask_sems.at[0], mask_sems.at[1], peer_rows[d], c).start()
    mask_buf[r] = mask[...]

    bias_exchange(0, 0)
    for k in range(1, CHUNKS):
        bias_chunk(k)
        bias_exchange(0, k)
    settle(parts_buf.at[pl.ds(0, cols - 1)], part_sems.at[1])
    load(CHUNKS + 5).wait()
    load(CHUNKS + 6).wait()
    total = jnp.zeros((width, tokens), jnp.float32)
    count_row = jnp.zeros((1, tokens), jnp.float32)
    for k in range(cols):
        total = total + lax.dot_general(
            atom_weight[...], parts_buf[k, 0:tokens], NT, preferred_element_type=jnp.float32
        )
        count_row = count_row + parts_buf[k, tokens : tokens + 16].astype(jnp.float32)[0:1]
    pooled[...] = total / count_row

    def in_desc(d, s):
        at = s + group * (side if d == 2 else 1 - side)
        return remote(
            first.at[at],
            stream.at[0, s, mine, c, side],
            in_sems.at[2, 0],
            in_sems.at[min(d, 2) - 1, s],
            peer_rows[d],
            c,
        )

    def start_sample(s):
        for k in range(2):
            at = s + group * k
            first[at] = (single[at].astype(jnp.float32) + pooled[...]).astype(jnp.bfloat16)
        stream[0, s, mine, c, side] = first[s + group * side]
        for d in (1, 2, 3):
            in_desc(d, s).start()

    def ag_desc(t, half, kind):
        l, s = lax.div(t, group), lax.rem(t, group)
        block = across if kind == 2 else c
        return remote(
            stream.at[l, s, half, block],
            stream.at[l, s, half, block],
            ag_sems.at[t, 4],
            ag_sems.at[t, 2 * half + kind % 2],
            r,
            across if kind == 1 else sibling,
        )

    def ag_arrived(t, half, kind):
        l, s = lax.div(t, group), lax.rem(t, group)
        held = stream.at[l, s, half, across] if kind else stream.at[l, s, half, pl.ds(0, 2)]
        settle(held, ag_sems.at[t, 2 * half + kind])

    def ag_send(t, half):
        ag_desc(t, half, 1).start()
        ag_desc(t, half, 0).start()

    def swap_desc(s):
        return remote(
            stream.at[1, s, mine, c],
            stream.at[1, s, mine, c],
            swap_sems.at[group],
            swap_sems.at[s],
            peer_rows[2],
            c,
        )

    def stage_first(t, half):
        if half is mine:
            settle(first.at[0], in_sems.at[0, t])
        else:
            settle(stream.at[0, t, other, c], in_sems.at[1, t])
        ag_send(t, half)

    def stage_next(t):
        s = lax.rem(t, group)
        settle(stream.at[1, s, other, c], swap_sems.at[s])
        ag_send(t, other)

    def forward(t, half):
        ag_arrived(t, half, 1)
        ag_desc(t, half, 2).start()

    score_scale = 1.0 / math.sqrt(HEAD_DIM)

    def normed_half(l, s, half):
        here = jnp.concatenate(
            [
                jnp.concatenate([stream[l, s, half, k, b] for k in range(cols)], axis=0)
                for b in range(2)
            ],
            axis=1,
        ).astype(jnp.float32)
        average = jnp.mean(here, axis=0, keepdims=True)
        centered = here - average
        variance = jnp.mean(centered * centered, axis=0, keepdims=True)
        return (centered * lax.rsqrt(variance + EPS)).astype(jnp.bfloat16)

    def project(t):
        l, s, slot = lax.div(t, group), lax.rem(t, group), lax.rem(t, 2)
        for half in (mine, other):
            ag_arrived(t, half, 0)
            here = normed_half(l, s, half)

            def rows_of(f, here=here):
                return jnp.dot(qkvg[l, f], here, preferred_element_type=jnp.float32)

            keys[slot, half] = rows_of(1).astype(jnp.bfloat16)
            values[slot, half] = rows_of(2).astype(jnp.bfloat16)
            if half is mine:
                query, gating = rows_of(0).T.astype(jnp.bfloat16), jax.nn.sigmoid(rows_of(3))
                for b in range(2):
                    queries[slot, b] = query[b * tokens : (b + 1) * tokens]
                    gates[slot, b] = gating[:, b * tokens : (b + 1) * tokens]

    def attend(t, blocks=None, kept=False):
        l, s, slot = lax.div(t, group), lax.rem(t, group), lax.rem(t, 2)
        live = jnp.concatenate([mask_buf[k] for k in range(rows)], axis=1) > 0
        square = lax.broadcasted_iota(jnp.int32, (tokens, tokens), 0) == lax.broadcasted_iota(
            jnp.int32, (tokens, tokens), 1
        )

        def one(h, b):
            at = slice(h * HEAD_DIM, (h + 1) * HEAD_DIM)
            key_here = jnp.concatenate([keys[slot, k, at] for k in range(2)], axis=1)
            value_here = jnp.concatenate([values[slot, k, at] for k in range(2)], axis=1)
            scores = (
                jnp.dot(queries[slot, b, :, at], key_here, preferred_element_type=jnp.float32)
                * score_scale
            )
            head_bias = jnp.concatenate([spread[l, b, k, h] for k in range(cols)], axis=1)
            scores = scores + head_bias.astype(jnp.float32)
            scores = jnp.where(live, scores, MASKED)
            highest = jnp.max(scores, axis=-1, keepdims=True)
            exponent = jnp.exp(scores - highest)
            summed = jnp.sum(exponent, axis=-1, keepdims=True)
            mixed = lax.dot_general(
                value_here,
                exponent.astype(jnp.bfloat16),
                NT,
                preferred_element_type=jnp.float32,
            )
            summed_row = jnp.sum(jnp.where(square, summed, 0.0), axis=0, keepdims=True)
            attended = mixed * (1.0 / summed_row)
            gated[l, s, b, c, at] = (gates[slot, b, at] * attended).astype(jnp.bfloat16)

        if blocks is not None:
            for b in blocks:
                for h in range(heads):
                    one(h, b)
                gated_desc(t, 1, b, kept).start()
                gated_desc(t, 0, b, kept).start()
        else:
            for h in range(heads):
                for b in range(2):
                    one(h, b)
            gated_desc(t, 1).start()
            gated_desc(t, 0).start()

    def gated_desc(t, kind, b=None, kept=False):
        l, s = lax.div(t, group), lax.rem(t, group)
        block = across if kind == 2 else c
        held = gated.at[l, s, :, block] if b is None else gated.at[l, s, b, block]
        return remote(
            held,
            held,
            gated_sems.at[2, 0, 0],
            gated_sems.at[kind % 2, b if kept else 0, t],
            r,
            across if kind == 1 else sibling,
        )

    def end_desc(s):
        return remote(
            final.at[s, 1 - side],
            out.at[side * group + s],
            end_sems.at[0],
            end_sems.at[1],
            near,
            c,
        )

    def pass_gated(t):
        l, s = lax.div(t, group), lax.rem(t, group)
        settle(gated.at[l, s, :, across], gated_sems.at[1, 0, t])
        gated_desc(t, 2).start()

    def pass_last(t, b):
        l, s = LAYERS - 1, lax.rem(t, group)
        settle(gated.at[l, s, b, across], gated_sems.at[1, b, t])
        gated_desc(t, 2, b, True).start()

    def finish_last(t, b):
        l, s = LAYERS - 1, lax.rem(t, group)
        settle(gated.at[l, s, b, pl.ds(0, 2)], gated_sems.at[0, b, t])
        joined = jnp.concatenate([gated[l, s, b, k] for k in range(cols)], axis=0)
        update = jnp.dot(out_w[l], joined, preferred_element_type=jnp.float32)
        return (stream[l, s, mine, c, b].astype(jnp.float32) + update).astype(jnp.bfloat16)

    def finish(t):
        l, s = lax.div(t, group), lax.rem(t, group)
        settle(gated.at[l, s, :, pl.ds(0, 2)], gated_sems.at[0, 0, t])
        joined = jnp.concatenate(
            [
                jnp.concatenate([gated[l, s, b, k] for k in range(cols)], axis=0)
                for b in range(2)
            ],
            axis=1,
        )
        update = jnp.dot(out_w[l], joined, preferred_element_type=jnp.float32)
        for b in range(2):
            cut = slice(b * tokens, (b + 1) * tokens)
            before = stream[l, s, mine, c, b].astype(jnp.float32)
            final[s, b] = (before + update[:, cut]).astype(jnp.bfloat16)

        @pl.when(l + 1 < LAYERS)
        def _():
            stream[1, s, mine, c] = final[s]
            swap_desc(s).start()
            ag_send(t + group, mine)

        @pl.when(l + 1 == LAYERS)
        def _():
            end_desc(s).start()
            out[side * group + s] = final[s, side]

    start_sample(0)
    for k in range(CHUNKS - 2):
        bias_pass(0, k)
        if k == 0:
            start_sample(1)
    stage_first(0, mine)
    bias_pass(0, CHUNKS - 2)
    stage_first(0, other)
    bias_pass(0, CHUNKS - 1)
    start_sample(2)
    stage_first(1, mine)
    forward(0, mine)
    stage_first(1, other)
    for k in range(CHUNKS):
        bias_exchange(1, k)
    settle(mask_buf.at[pl.ds(0, rows - 1)], mask_sems.at[1])
    load(CHUNKS + 7).wait()
    load(CHUNKS + 8).wait()

    def begin(t, carry):
        @pl.when(t > 0)
        def _():
            forward(t, mine)

        forward(t, other)
        project(t)
        attend(t, (side,))
        return carry

    def complete(t, carry):
        attend(t, (1 - side,))
        return carry

    lax.fori_loop(0, 2, begin, 0)
    bias_arrived(0)
    for s in range(3, group):
        start_sample(s)
    lax.fori_loop(0, 2, complete, 0)
    stage_first(2, mine)
    stage_first(2, other)
    for k in range(CHUNKS // 2):
        bias_pass(1, k)
    pass_gated(jnp.int32(0))
    forward(2, mine)
    finish(jnp.int32(0))
    for s in range(3, group):
        stage_first(s, mine)
        stage_first(s, other)
    forward(2, other)

    def step(t, carry):
        project(t)

        for k in range(CHUNKS // 2, CHUNKS):

            @pl.when(t == min(k, group - 1))
            def _(k=k):
                bias_pass(1, k)

        @pl.when(t == group)
        def _():
            bias_arrived(1)

        attend(t)
        pass_gated(t - 1)
        forward(t + 1, mine)

        @pl.when(t <= group)
        def _():
            finish(t - 1)

        @pl.when(t >= group + 2)
        def _():
            finish(t - 2)

        @pl.when((t + 2 >= group) & (t + 2 < tasks))
        def _():
            stage_next(t + 2)

        forward(t + 1, other)
        return carry

    lax.fori_loop(2, tasks - 1, step, 0)
    final_task = jnp.int32(tasks - 1)
    project(final_task)
    attend(final_task, (1 - side, side), True)
    pass_gated(final_task - 1)
    for k in (2, 1):
        finish(final_task - k)
    for b in (1 - side, side):
        pass_last(final_task, b)
    final[group - 1, 1 - side] = finish_last(final_task, 1 - side)
    end_desc(group - 1).start()
    out[side * group + group - 1] = finish_last(final_task, side)

    settle(out.at[pl.ds((1 - side) * group, group)], end_sems.at[1])
    settle(parts_buf.at[pl.ds(0, cols - 1)], part_sems.at[0])
    settle(mask_buf.at[pl.ds(0, rows - 1)], mask_sems.at[0])
    for l in range(LAYERS):
        settle(spread.at[l, 0, pl.ds(0, cols - 1)], a2a_sems.at[l, CHUNKS])
        settle(spread.at[l, 0], pair_sems.at[0, l])
    settle(stream.at[0, pl.ds(0, group), 0, pl.ds(0, 3), 0], in_sems.at[2, 0])
    settle(stream.at[1, pl.ds(0, group), 0, 0], swap_sems.at[group])
    settle(gated.at[:, :, :, pl.ds(0, 3)], gated_sems.at[2, 0, 0])
    settle(out.at[pl.ds(0, group)], end_sems.at[0])

    def drain(t, carry):
        settle(stream.at[0, 0, :, pl.ds(0, 3)], ag_sems.at[t, 4])
        return carry

    lax.fori_loop(0, tasks, drain, 0)


def pair_normed(rows_in):
    chans = rows_in.shape[1]
    if chans & (chans - 1):
        return layer_norm(rows_in.astype(jnp.float32)).astype(jnp.bfloat16)
    share = jnp.full((chans, chans), 1.0 / chans, jnp.bfloat16)
    average = jnp.dot(rows_in, share, preferred_element_type=jnp.float32)
    centered = rows_in.astype(jnp.float32) - average
    square = centered * centered
    variance = jnp.dot(square.astype(jnp.bfloat16), share, preferred_element_type=jnp.float32)
    return (centered * lax.rsqrt(variance + EPS)).astype(jnp.bfloat16)


def per_device_fused(
    rows,
    cols,
    single,
    pair_act,
    token_mask,
    atom_feats,
    atom_token,
    atom_count,
    atom_weight,
    bias_weight,
    qkvg_weight,
    out_weight,
):
    samples, tokens, width = single.shape
    single = single.transpose(0, 2, 1)
    group = samples // 2
    heads = width // HEAD_DIM
    chans = atom_feats.shape[1]
    slots = atom_feats.shape[0]
    pairs = pair_act.shape[2]
    all_heads = bias_weight.shape[1] * bias_weight.shape[2]
    bf16, f32 = jnp.bfloat16, jnp.float32
    dma = pltpu.SemaphoreType.DMA
    updated = pl.pallas_call(
        lambda *refs: fused(rows, cols, *refs),
        out_shape=jax.ShapeDtypeStruct(single.shape, bf16),
        in_specs=[pl.BlockSpec(memory_space=pl.ANY)] * 10,
        out_specs=pl.BlockSpec(memory_space=pltpu.VMEM),
        scratch_shapes=[
            pltpu.VMEM(pair_act.shape, bf16),
            pltpu.VMEM((all_heads, pairs), bf16),
            pltpu.VMEM(single.shape, bf16),
            pltpu.VMEM(atom_feats.shape, bf16),
            pltpu.VMEM((1, slots), jnp.int32),
            pltpu.VMEM((1, 1), jnp.int32),
            pltpu.VMEM((width, chans), bf16),
            pltpu.VMEM((1, tokens), jnp.int32),
            pltpu.VMEM(qkvg_weight.shape, bf16),
            pltpu.VMEM(out_weight.shape, bf16),
            pltpu.VMEM((LAYERS, cols, heads, tokens, tokens), bf16),
            pltpu.VMEM((LAYERS, 2, cols, heads, tokens, tokens), bf16),
            pltpu.VMEM((LAYERS, group, 2, cols, 2, width, tokens), bf16),
            pltpu.VMEM((samples, width, tokens), bf16),
            pltpu.VMEM((cols, tokens + 16, chans), bf16),
            pltpu.VMEM((width, tokens), f32),
            pltpu.VMEM((rows, 1, tokens), jnp.int32),
            pltpu.VMEM((2, 2, tokens, width), bf16),
            pltpu.VMEM((2, 2, width, 2 * tokens), bf16),
            pltpu.VMEM((2, 2, width, 2 * tokens), bf16),
            pltpu.VMEM((2, 2, width, tokens), f32),
            pltpu.VMEM((LAYERS, group, 2, cols, width, tokens), bf16),
            pltpu.VMEM((group, 2, width, tokens), bf16),
            dma((2,)),
            dma((2,)),
            dma((LAYERS, CHUNKS + 1)),
            dma((2, LAYERS)),
            dma((3, group)),
            dma((LAYERS * group, 5)),
            dma((group + 1,)),
            dma((3, 2, LAYERS * group)),
            dma((2,)),
            dma((CHUNKS + 9,)),
        ],
        compiler_params=pltpu.CompilerParams(
            collective_id=0, has_side_effects=True, vmem_limit_bytes=56 * 1024 * 1024
        ),
        name="fused_blocks",
    )(
        pair_act,
        bias_weight.reshape(pairs, all_heads).T,
        single,
        atom_feats,
        atom_token.reshape(1, slots),
        atom_count.reshape(1, 1),
        atom_weight.T,
        token_mask.reshape(1, tokens),
        qkvg_weight,
        out_weight,
    )
    return updated.transpose(0, 2, 1)


def solution(mesh):
    rows, cols = mesh.shape["row"], mesh.shape["col"]
    placed = (
        P(None, ("parts", "row"), "col"),
        P(("parts", "row"), "col", None),
        P(("parts", "row")),
        P(("parts", "row", "col"), None),
        P(("parts", "row", "col")),
        P(("parts", "row", "col")),
        P(None, "col"),
        P(),
        P(None, None, "col", None),
        P(None, "col", None),
    )

    def body(single, *rest):
        pairs = rest[0].shape
        square = rows == cols == 4 and single.shape[0] % 4 == 0 and pairs[0] == pairs[1]
        square = square and pairs[0] % 128 == 0
        if square and single.shape[2] % HEAD_DIM == 0:
            return per_device_fused(rows, cols, single, *rest)
        return per_device(single, *rest)

    return jax.shard_map(
        body,
        mesh=mesh,
        in_specs=placed,
        out_specs=P(None, ("parts", "row"), "col"),
        check_vma=False,
    )
```

```python
import math

import jax
import jax.numpy as jnp
from jax import lax
from jax.experimental import pallas as pl
from jax.experimental.pallas import tpu as pltpu
from jax.sharding import PartitionSpec as P

HEAD_DIM = 48
LAYERS = 2
CHUNKS = 4


EPS = 1e-05
MASKED = -1000000000.0
START_LOW = -1e30


def layer_norm(values):
    average = jnp.mean(values, axis=-1, keepdims=True)
    centered = values - average
    variance = jnp.mean(centered * centered, axis=-1, keepdims=True)
    return centered * lax.rsqrt(variance + EPS)


def per_device(
    single,
    pair_act,
    token_mask,
    atom_feats,
    atom_token,
    atom_count,
    atom_weight,
    bias_weight,
    qkvg_weight,
    out_weight,
):
    tok_rows = single.shape[1]
    sample_count = single.shape[0]
    slot_ids = jnp.arange(atom_feats.shape[0], dtype=jnp.int32)
    live_slots = slot_ids < atom_count[0]
    token_ids = jnp.arange(tok_rows, dtype=jnp.int32)
    owner_match = (token_ids[:, None] == atom_token[None, :]) & live_slots[None, :]
    owners = owner_match.astype(jnp.float32)
    counts = jnp.sum(owners, axis=1)
    atom_sums = jnp.dot(
        owner_match.astype(jnp.bfloat16), atom_feats, preferred_element_type=jnp.float32
    )
    sum_total, count_total = (
        lax.psum(atom_sums.astype(jnp.bfloat16), "col").astype(jnp.float32),
        lax.psum(counts[:, None].astype(jnp.bfloat16), "col").astype(jnp.float32),
    )
    pooled = (
        jnp.dot(sum_total, atom_weight.astype(jnp.float32), precision=lax.Precision.HIGHEST)
        / count_total
    )
    stream = (single.astype(jnp.float32) + pooled[None]).astype(jnp.bfloat16)
    pair_normed = layer_norm(pair_act.astype(jnp.float32)).astype(jnp.bfloat16)
    biases = jnp.einsum(
        "ijc,clh->lhij", pair_normed, bias_weight, preferred_element_type=jnp.float32
    ).astype(jnp.bfloat16)
    live_keys = (token_mask > 0).astype(jnp.bfloat16)[None, :]
    score_scale = 1.0 / math.sqrt(HEAD_DIM)
    for layer_idx in range(LAYERS):
        spread = lax.all_to_all(biases[layer_idx], "col", split_axis=0, concat_axis=2, tiled=True)
        gathered = lax.all_gather(stream, "col", axis=2, tiled=True)
        normed = layer_norm(gathered.astype(jnp.float32)).astype(jnp.bfloat16)
        projected = jnp.einsum(
            "std,fed->fste", normed, qkvg_weight[layer_idx], preferred_element_type=jnp.float32
        )
        head_width = projected.shape[3]
        heads_here = head_width // HEAD_DIM
        queries = (
            projected[0].astype(jnp.bfloat16).reshape(sample_count, tok_rows, heads_here, HEAD_DIM)
        )
        key_rows = projected[1].astype(jnp.bfloat16)
        value_rows = projected[2].astype(jnp.bfloat16)
        gating = jax.nn.sigmoid(projected[3])

        def attend(running, incoming, offset, queries=queries, spread=spread):
            top_old, summed_old, acc_old = running
            keys_in, values_in, live_in = incoming
            key_count = keys_in.shape[1]
            keys_heads = keys_in.reshape(sample_count, key_count, heads_here, HEAD_DIM)
            values_heads = values_in.reshape(sample_count, key_count, heads_here, HEAD_DIM)
            scores = (
                jnp.einsum(
                    "sqhd,skhd->shqk", queries, keys_heads, preferred_element_type=jnp.float32
                )
                * score_scale
            )
            scores = scores + spread.astype(jnp.float32)[None]
            scores = jnp.where(live_in[0][None, None, None, :] > 0, scores, MASKED)
            top_new = jnp.maximum(top_old, jnp.max(scores, axis=-1))
            exponent = jnp.exp(scores - top_new[..., None])
            summed_new = jnp.sum(exponent, axis=-1)
            weights = exponent.astype(jnp.bfloat16)
            acc_new = jnp.einsum(
                "shqk,skhd->shqd", weights, values_heads, preferred_element_type=jnp.float32
            )
            return (top_new, summed_new, acc_new)

        start_state = (
            jnp.full((sample_count, heads_here, tok_rows), START_LOW, jnp.float32),
            jnp.zeros((sample_count, heads_here, tok_rows), jnp.float32),
            jnp.zeros((sample_count, heads_here, tok_rows, HEAD_DIM), jnp.float32),
        )
        top_end, summed_end, acc_end = attend(
            start_state,
            (
                lax.all_gather(key_rows, "row", axis=1, tiled=True),
                lax.all_gather(value_rows, "row", axis=1, tiled=True),
                lax.all_gather(live_keys, "row", axis=1, tiled=True),
            ),
            jnp.int32(0),
        )
        attended = acc_end / summed_end[..., None]
        attended = attended.transpose(0, 2, 1, 3).reshape(sample_count, tok_rows, head_width)
        gated = (gating * attended).astype(jnp.bfloat16)
        out_rows = out_weight[layer_idx]

        def project(summed, incoming, offset, out_rows=out_rows):
            return jnp.einsum("std,ed->ste", incoming, out_rows, preferred_element_type=jnp.float32)

        zero_update = jnp.zeros((sample_count, tok_rows, out_rows.shape[0]), jnp.float32)
        update = project(
            zero_update, lax.all_gather(gated, "col", axis=2, tiled=True), jnp.int32(0)
        )
        stream = (stream.astype(jnp.float32) + update).astype(jnp.bfloat16)
    return stream


MESH = pl.DeviceIdType.MESH
NT = (((1,), (1,)), ((), ()))


def remote(src, dst, send_sem, recv_sem, row, col):
    return pltpu.make_async_remote_copy(
        src_ref=src,
        dst_ref=dst,
        send_sem=send_sem,
        recv_sem=recv_sem,
        device_id={"row": row, "col": col},
        device_id_type=MESH,
    )


def fused(
    rows,
    cols,
    pair_hbm,
    bias_w_hbm,
    single_hbm,
    feats_hbm,
    slot_token_hbm,
    slot_count_hbm,
    atom_weight_hbm,
    mask_hbm,
    qkvg_hbm,
    out_w_hbm,
    out,
    pair,
    bias_w,
    single,
    feats,
    slot_token,
    slot_count,
    atom_weight,
    mask,
    qkvg,
    out_w,
    bias,
    spread,
    stream,
    first,
    parts_buf,
    pooled,
    mask_buf,
    queries,
    keys,
    values,
    gates,
    gated,
    final,
    part_sems,
    mask_sems,
    a2a_sems,
    pair_sems,
    in_sems,
    ag_sems,
    swap_sems,
    gated_sems,
    end_sems,
    load_sems,
):
    r = lax.axis_index("row")
    c = lax.axis_index("col")
    samples, width, tokens = single.shape
    group = samples // 2
    tasks = LAYERS * group
    full = width * cols
    heads = width // HEAD_DIM
    sibling = c + 1 - 2 * lax.rem(c, 2)
    across = lax.rem(c + 2, cols)
    side = lax.rem(r, 2)
    mine = lax.div(r, 2)
    other = 1 - mine
    near = r + 1 - 2 * side
    peer_rows = {1: near, 2: lax.rem(r + 2, rows), 3: lax.rem(near + 2, rows)}

    lines = tokens // CHUNKS

    small = (
        (feats_hbm, feats),
        (slot_token_hbm, slot_token),
        (slot_count_hbm, slot_count),
        (bias_w_hbm, bias_w),
        (mask_hbm, mask),
        (atom_weight_hbm, atom_weight),
        (single_hbm, single),
        (qkvg_hbm, qkvg),
        (out_w_hbm, out_w),
    )

    def load(k):
        if k < CHUNKS:
            at = pl.ds(k * lines, lines)
            return pltpu.make_async_copy(pair_hbm.at[at], pair.at[at], load_sems.at[k])
        src, dst = small[k - CHUNKS]
        return pltpu.make_async_copy(src, dst, load_sems.at[k])

    for k in (0, *range(CHUNKS, CHUNKS + 5), *range(1, CHUNKS), *range(CHUNKS + 5, CHUNKS + 9)):
        load(k).start()

    barrier = pltpu.get_barrier_semaphore()
    for dc in range(1, cols):
        pl.semaphore_signal(
            barrier,
            inc=1,
            device_id={"row": r, "col": lax.rem(c + dc, cols)},
            device_id_type=MESH,
        )
    for d in range(1, rows):
        pl.semaphore_signal(
            barrier, inc=1, device_id={"row": peer_rows[d], "col": c}, device_id_type=MESH
        )
    def col_of(d):
        return lax.rem(c + d, cols)

    def rows_at(k):
        return pl.ds(k * lines, lines)

    def bias_chunk(k):
        load(k).wait()
        here = pair_normed(pair[rows_at(k)].reshape(lines * tokens, pair.shape[2]))
        made = lax.dot_general(bias_w[...], here, NT, preferred_element_type=jnp.float32)
        made = made.astype(jnp.bfloat16).reshape(LAYERS, cols, heads, lines, tokens)
        bias[:, :, :, rows_at(k)] = made

    def settle(ref, sem):
        pltpu.make_async_copy(ref, ref, sem).wait()

    def a2a_desc(l, d, k):
        to = col_of(d)
        return remote(
            bias.at[l, to, :, rows_at(k)],
            spread.at[l, side, c, :, rows_at(k)],
            a2a_sems.at[l, CHUNKS],
            a2a_sems.at[l, k],
            r,
            to,
        )

    def pair_desc(l, d, k):
        block = col_of(cols - d) if d else c
        held = spread.at[l, side, block, :, rows_at(k)]
        return remote(
            held if d else bias.at[l, c, :, rows_at(k)],
            held,
            pair_sems.at[0, l],
            pair_sems.at[1, l],
            near,
            c,
        )

    def bias_exchange(l, k):
        for d in (2, 3, 1):
            a2a_desc(l, d, k).start()
        if l == 0:
            pair_desc(l, 0, k).start()
        spread[l, side, c, :, rows_at(k)] = bias[l, c, :, rows_at(k)]

    def bias_pass(l, k):
        if l:
            pair_desc(l, 0, k).start()
        settle(spread.at[l, side, pl.ds(0, cols - 1), :, rows_at(k)], a2a_sems.at[l, k])
        for d in range(1, cols):
            pair_desc(l, d, k).start()

    def bias_arrived(l):
        settle(spread.at[l, 1 - side], pair_sems.at[1, l])

    slots = feats.shape[0]
    for k in range(5):
        load(CHUNKS + k).wait()
    token_ids = lax.broadcasted_iota(jnp.int32, (tokens, slots), 0)
    slot_ids = lax.broadcasted_iota(jnp.int32, (tokens, slots), 1)
    match = (token_ids == slot_token[...]) & (slot_ids < slot_count[...])
    owners = jnp.where(match, 1.0, 0.0).astype(jnp.bfloat16)
    parts_buf[c, 0:tokens] = jnp.dot(
        owners, feats[...], preferred_element_type=jnp.float32
    ).astype(jnp.bfloat16)
    parts_buf[c, tokens : tokens + 16] = lax.dot_general(
        jnp.ones((16, slots), jnp.bfloat16), owners, NT, preferred_element_type=jnp.float32
    ).astype(jnp.bfloat16)
    bias_chunk(0)
    pl.semaphore_wait(barrier, cols - 1 + rows - 1)
    for d in range(1, cols):
        remote(
            parts_buf.at[c], parts_buf.at[c], part_sems.at[0], part_sems.at[1], r, col_of(d)
        ).start()
    for d in range(1, rows):
        remote(mask, mask_buf.at[r], mask_sems.at[0], mask_sems.at[1], peer_rows[d], c).start()
    mask_buf[r] = mask[...]

    bias_exchange(0, 0)
    for k in range(1, CHUNKS):
        bias_chunk(k)
        bias_exchange(0, k)
    settle(parts_buf.at[pl.ds(0, cols - 1)], part_sems.at[1])
    load(CHUNKS + 5).wait()
    load(CHUNKS + 6).wait()
    total = jnp.zeros((width, tokens), jnp.float32)
    count_row = jnp.zeros((1, tokens), jnp.float32)
    for k in range(cols):
        total = total + lax.dot_general(
            atom_weight[...], parts_buf[k, 0:tokens], NT, preferred_element_type=jnp.float32
        )
        count_row = count_row + parts_buf[k, tokens : tokens + 16].astype(jnp.float32)[0:1]
    pooled[...] = total / count_row

    def in_desc(d, s):
        at = s + group * (side if d == 2 else 1 - side)
        return remote(
            first.at[at],
            stream.at[0, s, mine, c, side],
            in_sems.at[2, 0],
            in_sems.at[min(d, 2) - 1, s],
            peer_rows[d],
            c,
        )

    def start_sample(s):
        for k in range(2):
            at = s + group * k
            first[at] = (single[at].astype(jnp.float32) + pooled[...]).astype(jnp.bfloat16)
        stream[0, s, mine, c, side] = first[s + group * side]
        for d in (1, 2, 3):
            in_desc(d, s).start()

    def ag_desc(t, half, kind):
        l, s = lax.div(t, group), lax.rem(t, group)
        block = across if kind == 2 else c
        return remote(
            stream.at[l, s, half, block],
            stream.at[l, s, half, block],
            ag_sems.at[t, 4],
            ag_sems.at[t, 2 * half + kind % 2],
            r,
            across if kind == 1 else sibling,
        )

    def ag_arrived(t, half, kind):
        l, s = lax.div(t, group), lax.rem(t, group)
        held = stream.at[l, s, half, across] if kind else stream.at[l, s, half, pl.ds(0, 2)]
        settle(held, ag_sems.at[t, 2 * half + kind])

    def ag_send(t, half):
        ag_desc(t, half, 1).start()
        ag_desc(t, half, 0).start()

    def swap_desc(s):
        return remote(
            stream.at[1, s, mine, c],
            stream.at[1, s, mine, c],
            swap_sems.at[group],
            swap_sems.at[s],
            peer_rows[2],
            c,
        )

    def stage_first(t, half):
        if half is mine:
            settle(first.at[0], in_sems.at[0, t])
        else:
            settle(stream.at[0, t, other, c], in_sems.at[1, t])
        ag_send(t, half)

    def stage_next(t):
        s = lax.rem(t, group)
        settle(stream.at[1, s, other, c], swap_sems.at[s])
        ag_send(t, other)

    def forward(t, half):
        ag_arrived(t, half, 1)
        ag_desc(t, half, 2).start()

    score_scale = 1.0 / math.sqrt(HEAD_DIM)

    def normed_half(l, s, half):
        here = jnp.concatenate(
            [
                jnp.concatenate([stream[l, s, half, k, b] for k in range(cols)], axis=0)
                for b in range(2)
            ],
            axis=1,
        ).astype(jnp.float32)
        average = jnp.mean(here, axis=0, keepdims=True)
        centered = here - average
        variance = jnp.mean(centered * centered, axis=0, keepdims=True)
        return (centered * lax.rsqrt(variance + EPS)).astype(jnp.bfloat16)

    def project(t):
        l, s, slot = lax.div(t, group), lax.rem(t, group), lax.rem(t, 2)
        for half in (mine, other):
            ag_arrived(t, half, 0)
            here = normed_half(l, s, half)

            def rows_of(f, here=here):
                return jnp.dot(qkvg[l, f], here, preferred_element_type=jnp.float32)

            keys[slot, half] = rows_of(1).astype(jnp.bfloat16)
            values[slot, half] = rows_of(2).astype(jnp.bfloat16)
            if half is mine:
                query, gating = rows_of(0).T.astype(jnp.bfloat16), jax.nn.sigmoid(rows_of(3))
                for b in range(2):
                    queries[slot, b] = query[b * tokens : (b + 1) * tokens]
                    gates[slot, b] = gating[:, b * tokens : (b + 1) * tokens]

    def attend(t, blocks=None):
        l, s, slot = lax.div(t, group), lax.rem(t, group), lax.rem(t, 2)
        live = jnp.concatenate([mask_buf[k] for k in range(rows)], axis=1) > 0
        square = lax.broadcasted_iota(jnp.int32, (tokens, tokens), 0) == lax.broadcasted_iota(
            jnp.int32, (tokens, tokens), 1
        )

        def one(h, b):
            at = slice(h * HEAD_DIM, (h + 1) * HEAD_DIM)
            key_here = jnp.concatenate([keys[slot, k, at] for k in range(2)], axis=1)
            value_here = jnp.concatenate([values[slot, k, at] for k in range(2)], axis=1)
            scores = (
                jnp.dot(queries[slot, b, :, at], key_here, preferred_element_type=jnp.float32)
                * score_scale
            )
            head_bias = jnp.concatenate([spread[l, b, k, h] for k in range(cols)], axis=1)
            scores = scores + head_bias.astype(jnp.float32)
            scores = jnp.where(live, scores, MASKED)
            highest = jnp.max(scores, axis=-1, keepdims=True)
            exponent = jnp.exp(scores - highest)
            summed = jnp.sum(exponent, axis=-1, keepdims=True)
            mixed = lax.dot_general(
                value_here,
                exponent.astype(jnp.bfloat16),
                NT,
                preferred_element_type=jnp.float32,
            )
            summed_row = jnp.sum(jnp.where(square, summed, 0.0), axis=0, keepdims=True)
            attended = mixed * (1.0 / summed_row)
            gated[l, s, b, c, at] = (gates[slot, b, at] * attended).astype(jnp.bfloat16)

        if blocks is not None:
            for i, b in enumerate(blocks):
                for h in range(heads):
                    one(h, b)
                gated_desc(t, 1, b, i).start()
                gated_desc(t, 0, b, i).start()
        else:
            for h in range(heads):
                for b in range(2):
                    one(h, b)
            gated_desc(t, 1).start()
            gated_desc(t, 0).start()

    def gated_sem(t, kind, second):
        return gated_sems.at[2, 1 + kind] if second else gated_sems.at[kind, t]

    def gated_desc(t, kind, b=None, second=0):
        l, s = lax.div(t, group), lax.rem(t, group)
        block = across if kind == 2 else c
        held = gated.at[l, s, :, block] if b is None else gated.at[l, s, b, block]
        return remote(
            held,
            held,
            gated_sems.at[2, 0],
            gated_sem(t, kind % 2, second),
            r,
            across if kind == 1 else sibling,
        )

    def end_desc(s):
        return remote(
            final.at[s, 1 - side],
            out.at[side * group + s],
            end_sems.at[0],
            end_sems.at[1],
            near,
            c,
        )

    def pass_gated(t):
        l, s = lax.div(t, group), lax.rem(t, group)
        settle(gated.at[l, s, :, across], gated_sem(t, 1, 0))
        gated_desc(t, 2).start()

    def pass_last(t, b, second):
        l, s = LAYERS - 1, lax.rem(t, group)
        settle(gated.at[l, s, b, across], gated_sem(t, 1, second))
        gated_desc(t, 2, b, second).start()

    def finish_last(t, b, second):
        l, s = LAYERS - 1, lax.rem(t, group)
        settle(gated.at[l, s, b, pl.ds(0, 2)], gated_sem(t, 0, second))
        joined = jnp.concatenate([gated[l, s, b, k] for k in range(cols)], axis=0)
        update = jnp.dot(out_w[l], joined, preferred_element_type=jnp.float32)
        return (stream[l, s, mine, c, b].astype(jnp.float32) + update).astype(jnp.bfloat16)

    def finish(t):
        l, s = lax.div(t, group), lax.rem(t, group)
        settle(gated.at[l, s, :, pl.ds(0, 2)], gated_sem(t, 0, 0))
        joined = jnp.concatenate(
            [
                jnp.concatenate([gated[l, s, b, k] for k in range(cols)], axis=0)
                for b in range(2)
            ],
            axis=1,
        )
        update = jnp.dot(out_w[l], joined, preferred_element_type=jnp.float32)
        for b in range(2):
            cut = slice(b * tokens, (b + 1) * tokens)
            before = stream[l, s, mine, c, b].astype(jnp.float32)
            final[s, b] = (before + update[:, cut]).astype(jnp.bfloat16)

        @pl.when(l + 1 < LAYERS)
        def _():
            stream[1, s, mine, c] = final[s]
            swap_desc(s).start()
            ag_send(t + group, mine)

        @pl.when(l + 1 == LAYERS)
        def _():
            end_desc(s).start()
            out[side * group + s] = final[s, side]

    start_sample(0)
    start_sample(1)
    for k in range(CHUNKS - 2):
        bias_pass(0, k)
    stage_first(0, mine)
    bias_pass(0, CHUNKS - 2)
    stage_first(0, other)
    bias_pass(0, CHUNKS - 1)
    start_sample(2)
    stage_first(1, mine)
    forward(0, mine)
    stage_first(1, other)
    for k in range(CHUNKS):
        bias_exchange(1, k)
    settle(mask_buf.at[pl.ds(0, rows - 1)], mask_sems.at[1])
    load(CHUNKS + 7).wait()
    load(CHUNKS + 8).wait()

    def begin(t, carry):
        @pl.when(t > 0)
        def _():
            forward(t, mine)

        forward(t, other)
        project(t)
        attend(t, (side,))
        return carry

    def complete(t, carry):
        attend(t, (1 - side,))
        return carry

    lax.fori_loop(0, 2, begin, 0)
    bias_arrived(0)
    for s in range(3, group):
        start_sample(s)
    lax.fori_loop(0, 2, complete, 0)
    stage_first(2, mine)
    stage_first(2, other)
    for k in range(CHUNKS // 2):
        bias_pass(1, k)
    pass_gated(jnp.int32(0))
    forward(2, mine)
    finish(jnp.int32(0))
    for s in range(3, group):
        stage_first(s, mine)
        stage_first(s, other)
    forward(2, other)

    def step(t, carry):
        project(t)

        for k in range(CHUNKS // 2, CHUNKS):

            @pl.when(t == min(k, group - 1))
            def _(k=k):
                bias_pass(1, k)

        @pl.when(t == group)
        def _():
            bias_arrived(1)

        attend(t)
        pass_gated(t - 1)
        forward(t + 1, mine)

        @pl.when(t <= group)
        def _():
            finish(t - 1)

        @pl.when(t >= group + 2)
        def _():
            finish(t - 2)

        @pl.when((t + 2 >= group) & (t + 2 < tasks))
        def _():
            stage_next(t + 2)

        forward(t + 1, other)
        return carry

    lax.fori_loop(2, tasks - 1, step, 0)
    final_task = jnp.int32(tasks - 1)
    project(final_task)
    attend(final_task, (1 - side, side))
    pass_gated(final_task - 1)
    for k in (2, 1):
        finish(final_task - k)
    for i, b in enumerate((1 - side, side)):
        pass_last(final_task, b, i)
    final[group - 1, 1 - side] = finish_last(final_task, 1 - side, 0)
    end_desc(group - 1).start()
    out[side * group + group - 1] = finish_last(final_task, side, 1)

    settle(out.at[pl.ds((1 - side) * group, group)], end_sems.at[1])
    settle(parts_buf.at[pl.ds(0, cols - 1)], part_sems.at[0])
    settle(mask_buf.at[pl.ds(0, rows - 1)], mask_sems.at[0])
    for l in range(LAYERS):
        settle(spread.at[l, 0, pl.ds(0, cols - 1)], a2a_sems.at[l, CHUNKS])
        settle(spread.at[l, 0], pair_sems.at[0, l])
    settle(stream.at[0, pl.ds(0, group), 0, pl.ds(0, 3), 0], in_sems.at[2, 0])
    settle(stream.at[1, pl.ds(0, group), 0, 0], swap_sems.at[group])
    settle(gated.at[:, :, :, pl.ds(0, 3)], gated_sems.at[2, 0])
    settle(out.at[pl.ds(0, group)], end_sems.at[0])

    def drain(t, carry):
        settle(stream.at[0, 0, :, pl.ds(0, 3)], ag_sems.at[t, 4])
        return carry

    lax.fori_loop(0, tasks, drain, 0)


def pair_normed(rows_in):
    chans = rows_in.shape[1]
    if chans & (chans - 1):
        return layer_norm(rows_in.astype(jnp.float32)).astype(jnp.bfloat16)
    share = jnp.full((chans, chans), 1.0 / chans, jnp.bfloat16)
    average = jnp.dot(rows_in, share, preferred_element_type=jnp.float32)
    centered = rows_in.astype(jnp.float32) - average
    square = centered * centered
    variance = jnp.dot(square.astype(jnp.bfloat16), share, preferred_element_type=jnp.float32)
    return (centered * lax.rsqrt(variance + EPS)).astype(jnp.bfloat16)


def per_device_fused(
    rows,
    cols,
    single,
    pair_act,
    token_mask,
    atom_feats,
    atom_token,
    atom_count,
    atom_weight,
    bias_weight,
    qkvg_weight,
    out_weight,
):
    samples, tokens, width = single.shape
    single = single.transpose(0, 2, 1)
    group = samples // 2
    heads = width // HEAD_DIM
    chans = atom_feats.shape[1]
    slots = atom_feats.shape[0]
    pairs = pair_act.shape[2]
    all_heads = bias_weight.shape[1] * bias_weight.shape[2]
    bf16, f32 = jnp.bfloat16, jnp.float32
    dma = pltpu.SemaphoreType.DMA
    updated = pl.pallas_call(
        lambda *refs: fused(rows, cols, *refs),
        out_shape=jax.ShapeDtypeStruct(single.shape, bf16),
        in_specs=[pl.BlockSpec(memory_space=pl.ANY)] * 10,
        out_specs=pl.BlockSpec(memory_space=pltpu.VMEM),
        scratch_shapes=[
            pltpu.VMEM(pair_act.shape, bf16),
            pltpu.VMEM((all_heads, pairs), bf16),
            pltpu.VMEM(single.shape, bf16),
            pltpu.VMEM(atom_feats.shape, bf16),
            pltpu.VMEM((1, slots), jnp.int32),
            pltpu.VMEM((1, 1), jnp.int32),
            pltpu.VMEM((width, chans), bf16),
            pltpu.VMEM((1, tokens), jnp.int32),
            pltpu.VMEM(qkvg_weight.shape, bf16),
            pltpu.VMEM(out_weight.shape, bf16),
            pltpu.VMEM((LAYERS, cols, heads, tokens, tokens), bf16),
            pltpu.VMEM((LAYERS, 2, cols, heads, tokens, tokens), bf16),
            pltpu.VMEM((LAYERS, group, 2, cols, 2, width, tokens), bf16),
            pltpu.VMEM((samples, width, tokens), bf16),
            pltpu.VMEM((cols, tokens + 16, chans), bf16),
            pltpu.VMEM((width, tokens), f32),
            pltpu.VMEM((rows, 1, tokens), jnp.int32),
            pltpu.VMEM((2, 2, tokens, width), bf16),
            pltpu.VMEM((2, 2, width, 2 * tokens), bf16),
            pltpu.VMEM((2, 2, width, 2 * tokens), bf16),
            pltpu.VMEM((2, 2, width, tokens), f32),
            pltpu.VMEM((LAYERS, group, 2, cols, width, tokens), bf16),
            pltpu.VMEM((group, 2, width, tokens), bf16),
            dma((2,)),
            dma((2,)),
            dma((LAYERS, CHUNKS + 1)),
            dma((2, LAYERS)),
            dma((3, group)),
            dma((LAYERS * group, 5)),
            dma((group + 1,)),
            dma((3, LAYERS * group)),
            dma((2,)),
            dma((CHUNKS + 9,)),
        ],
        compiler_params=pltpu.CompilerParams(
            collective_id=0, has_side_effects=True, vmem_limit_bytes=56 * 1024 * 1024
        ),
        name="fused_blocks",
    )(
        pair_act,
        bias_weight.reshape(pairs, all_heads).T,
        single,
        atom_feats,
        atom_token.reshape(1, slots),
        atom_count.reshape(1, 1),
        atom_weight.T,
        token_mask.reshape(1, tokens),
        qkvg_weight,
        out_weight,
    )
    return updated.transpose(0, 2, 1)


def solution(mesh):
    rows, cols = mesh.shape["row"], mesh.shape["col"]
    placed = (
        P(None, ("parts", "row"), "col"),
        P(("parts", "row"), "col", None),
        P(("parts", "row")),
        P(("parts", "row", "col"), None),
        P(("parts", "row", "col")),
        P(("parts", "row", "col")),
        P(None, "col"),
        P(),
        P(None, None, "col", None),
        P(None, "col", None),
    )

    def body(single, *rest):
        pairs = rest[0].shape
        square = rows == cols == 4 and single.shape[0] % 4 == 0 and pairs[0] == pairs[1]
        square = square and pairs[0] % 128 == 0
        if square and single.shape[2] % HEAD_DIM == 0:
            return per_device_fused(rows, cols, single, *rest)
        return per_device(single, *rest)

    return jax.shard_map(
        body,
        mesh=mesh,
        in_specs=placed,
        out_specs=P(None, ("parts", "row"), "col"),
        check_vma=False,
    )
```
